32 devices in a mesh: group: 2 (over y), tile: 4 (over z), sect: 2 (over x), sub: 2 (over core).
Axes of the slice: x: 2, y: 2, z: 4, core: 2. Of those that a mesh axis runs over, the one named last changes fastest.
Arguments:
- air_state: float32 [4, 80, 64, 256], P(None, ('sect', 'sub'), ('group', 'tile')), parts along dimension 2, may hold values from -3 to 3
- fire_level: float32 [640, 2560], P(('group', 'tile'), ('sect', 'sub')), parts along dimension 0, may hold values from 0.2 to 3
- fuel_left: float32 [640, 2560], P(('group', 'tile'), ('sect', 'sub')), parts along dimension 0, may hold values from 0.3 to 1
- fuel_class: int32 [640, 2560], P(('group', 'tile'), ('sect', 'sub')), parts along dimension 0, may hold values from 0 to 12
- ignition: int32 [640, 2560], P(('group', 'tile'), ('sect', 'sub')), parts along dimension 0, may hold values from 0 to 4, as said below
- plan: int32 [4], replicated, may hold values from 1 to 3
- spread_rate: float32 [13], replicated, may hold values from 0.05 to 0.3
- burn_time: float32 [13], replicated, may hold values from 0.5 to 8
- heat_content: float32 [13], replicated, may hold values from 1 to 10
- moisture_content: float32 [13], replicated, may hold values from 0.1 to 1
Outputs:
- air_out: float32 [4, 80, 64, 256], P(None, ('sect', 'sub'), ('group', 'tile')), parts along dimension 2
- level_out: float32 [640, 2560], P(('group', 'tile'), ('sect', 'sub')), parts along dimension 0
- fuel_out: float32 [640, 2560], P(('group', 'tile'), ('sect', 'sub')), parts along dimension 0
The draws below stay inside these ranges and needn't reach their ends.
There are 2 independent parts, one for each index of `group`. The reference program is written for one: setup_inputs(seed, part) draws one part's arguments, and reference() takes and returns one part's arrays. A program takes and returns all parts, laid end to end along the dimension named above; an argument that names none is the same for every part. Nothing has to cross between parts.
Inputs may be any that keep to these rules, and one draw needn't show every extreme that they name: `ignition`: A cell with value c is ignited at the start of coupling step c; cells with value 4 are not ignited in the window. Ignited cells lie in scattered atmosphere columns. The plan is shared by all scenarios.
All inputs are finite; a program needn't handle non-finite values.
Results may differ from the reference program's by a relative error of at most 0.0001.
Values sent between devices are 32-bit elements; how exact they have to be, the bound alone decides.
A program may use at most 128 MiB of HBM per device.

```python
import math
import jax
import jax.numpy as jnp
import numpy as np
from jax import lax

LEVELS = 80
REFINE = 10
NFUEL = 13
STEPS = 4
SUBSTEPS = 4
NX = 32
NY = 256
FIRE_X = 320
FIRE_Y = 2560


def draw_ignition(key, part):
    first_key, second_key, third_key = jax.random.split(key, 3)
    active = jax.random.randint(first_key, (NX, NY), 0, 8) == 0
    ignite_at = jax.random.randint(second_key, (NX, NY), 0, STEPS)
    coarse_map = jnp.where(active, ignite_at, STEPS)
    fine_map = jnp.repeat(jnp.repeat(coarse_map, REFINE, axis=0), REFINE, axis=1)
    chosen = jax.random.randint(third_key, (FIRE_X, FIRE_Y), 0, 4) == 0
    return jnp.where(chosen, fine_map, STEPS).astype(jnp.int32)


def place_ends(values, rng, smallest, top_value):
    dims = values.shape
    place = [jax.random.randint(jax.random.fold_in(rng, axis), (), 0, dims[axis]) for axis in range(len(dims))]
    values = values.at[tuple(place)].set(smallest)
    longest = dims.index(max(dims))
    place[longest] = (place[longest] + 1) % dims[longest]
    return values.at[tuple(place)].set(top_value)


def levels(own_key, dims, shards, least, largest):
    def one(position, shards_of):
        steps = jax.random.uniform(jax.random.fold_in(jax.random.fold_in(own_key, 6), position), (shards_of,), jnp.float32, least / len(shards), largest / len(shards))
        return jnp.repeat(jnp.exp(steps), dims[position] // shards_of).reshape((-1,) + (1,) * (len(dims) - position - 1))

    loudness = one(*shards[0])
    for cut in shards[1:]:
        loudness = loudness * one(*cut)
    return loudness


def rank_table(count, lean):
    portions = [(1 << 20) // math.isqrt(grade ** lean) + 1 for grade in range(1, count + 1)]
    deviation = 1 + sum(portions) // (1 << 30)
    return np.cumsum(np.array([max(1, weight // deviation) for weight in portions]))


def ranked_ids(rng, dims, amount, lean):
    listing = rank_table(amount, lean)
    ticket = jax.random.randint(jax.random.fold_in(rng, 1), dims, 0, int(listing[amount - 1]))
    standing = jnp.searchsorted(jnp.asarray(listing, jnp.int32), ticket, side="right")
    return jax.random.permutation(jax.random.fold_in(rng, 2), amount)[standing].astype(jnp.int32)


def centred(own_key, extent, deviation, reach, cuts=(), dtype=jnp.bfloat16):
    drawn = deviation * jax.random.normal(own_key, extent, jnp.float32)
    if cuts:
        drawn = drawn * levels(own_key, extent, cuts, -0.22, 0.18)
    return jnp.clip(drawn, -reach, reach).astype(dtype)


def setup_inputs(seed: int = 0, part: int = 0) -> dict:
    arg_keys = jax.random.split(jax.random.key(seed), 11)
    own_keys = jax.random.split(jax.random.fold_in(arg_keys[10], part), 11)
    air_state = centred(own_keys[0], (4, LEVELS, NX, NY), 1.0, 3.0, ((1, 4), (2, 4)), jnp.float32)
    fire_level = jnp.clip(0.2 + 2.8 * jax.random.uniform(own_keys[1], (FIRE_X, FIRE_Y), jnp.float32) ** levels(own_keys[1], (FIRE_X, FIRE_Y), ((0, 4), (1, 4)), -0.2, 0.2), 0.2, 3.0)
    fuel_left = jnp.clip(0.3 + 0.7 * jax.random.uniform(own_keys[2], (FIRE_X, FIRE_Y), jnp.float32) ** levels(own_keys[2], (FIRE_X, FIRE_Y), ((0, 4), (1, 4)), -0.2, 0.2), 0.3, 1.0)
    fuel_class = place_ends(ranked_ids(own_keys[3], (FIRE_X, FIRE_Y), NFUEL, 2), jax.random.fold_in(own_keys[3], 3), 0, NFUEL - 1).astype(jnp.int32)
    ignition = draw_ignition(jax.random.fold_in(jax.random.fold_in(arg_keys[10], part), 71), part)
    plan = place_ends(jax.random.randint(arg_keys[5], (STEPS,), 1, 4), jax.random.fold_in(arg_keys[5], 1), 1, 3).astype(jnp.int32)
    spread_rate = jnp.clip(jnp.exp(jax.random.uniform(arg_keys[6], (NFUEL,), jnp.float32, math.log(0.05), math.log(0.3))), 0.05, 0.3)
    burn_time = jnp.clip(jnp.exp(jax.random.uniform(arg_keys[7], (NFUEL,), jnp.float32, math.log(0.5), math.log(8.0))), 0.5, 8.0)
    heat_content = jnp.clip(jnp.exp(jax.random.uniform(arg_keys[8], (NFUEL,), jnp.float32, math.log(1.0), math.log(10.0))), 1.0, 10.0)
    moisture_content = jnp.clip(jnp.exp(jax.random.uniform(arg_keys[9], (NFUEL,), jnp.float32, math.log(0.1), math.log(1.0))), 0.1, 1.0)
    return dict(air_state=air_state, fire_level=fire_level, fuel_left=fuel_left, fuel_class=fuel_class, ignition=ignition, plan=plan, spread_rate=spread_rate, burn_time=burn_time, heat_content=heat_content, moisture_content=moisture_content)


air_delta = 0.1
diffusion = 0.2
heat_gain = 20.0
vapour_gain = 20.0
lift_gain = 0.3
wind_gain = 0.5
fire_delta = 0.15

def level_weights(layer_count):
    height = jnp.arange(layer_count).astype(jnp.float32)
    profile = jnp.exp(-2.0 * height / layer_count)
    profile = layer_count * profile / jnp.sum(profile)
    column = jnp.exp(-height / layer_count)
    column = column / jnp.sum(column)
    return (profile, column)

def fire_core(padded, fuel_now, energy, vapour, rate_cell, burnout, heat_cell, moist_cell, wind_east, wind_north, fire_step):
    at_centre = padded[1:-1, 1:-1]
    at_west = padded[:-2, 1:-1]
    at_east = padded[2:, 1:-1]
    at_south = padded[1:-1, :-2]
    at_north = padded[1:-1, 2:]
    steepness = jnp.sqrt(jnp.maximum(at_centre - at_west, 0.0) ** 2 + jnp.minimum(at_east - at_centre, 0.0) ** 2 + jnp.maximum(at_centre - at_south, 0.0) ** 2 + jnp.minimum(at_north - at_centre, 0.0) ** 2)
    grad_east = 0.5 * (at_east - at_west)
    grad_north = 0.5 * (at_north - at_south)
    tailwind = (wind_east * grad_east + wind_north * grad_north) / jnp.sqrt(grad_east * grad_east + grad_north * grad_north + 1.0)
    fire_speed = rate_cell * (1.0 + wind_gain * jnp.maximum(tailwind, 0.0))
    level_set = at_centre - fire_step * fire_speed * steepness
    burning = jnp.clip(0.5 - level_set, 0.0, 1.0)
    remain = fuel_now * jnp.exp(-fire_step * burning / burnout)
    consumed = fuel_now - remain
    return (level_set, remain, energy + consumed * heat_cell, vapour + consumed * moist_cell)

def air_core(padded, flux_coarse, profile):
    at_centre = padded[:, 1:-1, 1:-1, 1:-1]
    at_below = padded[:, :-2, 1:-1, 1:-1]
    at_above = padded[:, 2:, 1:-1, 1:-1]
    at_west = padded[:, 1:-1, :-2, 1:-1]
    at_east = padded[:, 1:-1, 2:, 1:-1]
    at_south = padded[:, 1:-1, 1:-1, :-2]
    at_north = padded[:, 1:-1, 1:-1, 2:]
    speed_east = at_centre[2]
    speed_north = at_centre[3]
    advect = jnp.maximum(speed_east, 0.0) * (at_centre - at_west) + jnp.minimum(speed_east, 0.0) * (at_east - at_centre) + jnp.maximum(speed_north, 0.0) * (at_centre - at_south) + jnp.minimum(speed_north, 0.0) * (at_north - at_centre)
    diffused = at_west + at_east + at_south + at_north + at_below + at_above - 6.0 * at_centre
    lift_east = at_east[0] + 0.6 * at_east[1] - (at_west[0] + 0.6 * at_west[1])
    lift_north = at_north[0] + 0.6 * at_north[1] - (at_south[0] + 0.6 * at_south[1])
    heights = profile[:, None, None]
    forcing = jnp.stack([heat_gain * flux_coarse[0][None] * heights, vapour_gain * flux_coarse[1][None] * heights, 0.5 * lift_gain * lift_east, 0.5 * lift_gain * lift_north])
    return at_centre + air_delta * (diffusion * diffused - advect + forcing)

def coarsen(fine_field, refine_by):
    channels, row_count, col_count = fine_field.shape
    blocks = fine_field.reshape(channels, row_count // refine_by, refine_by, col_count // refine_by, refine_by)
    return lax.optimization_barrier(jnp.sum(blocks, axis=(2, 4))) / (refine_by * refine_by)

def reference(air_state, fire_level, fuel_left, fuel_class, ignition, plan, spread_rate, burn_time, heat_content, moisture_content):
    rate_cell = spread_rate[fuel_class]
    burnout = burn_time[fuel_class]
    heat_cell = heat_content[fuel_class]
    moist_cell = moisture_content[fuel_class]
    profile, column = level_weights(LEVELS)
    air_field = air_state
    level_set = fire_level
    fuel_now = fuel_left
    for coupling in range(STEPS):
        wind_coarse = lax.optimization_barrier(jnp.sum(column[None, :, None, None] * air_field[2:4], axis=1))
        wind_fine = jnp.repeat(jnp.repeat(wind_coarse, REFINE, axis=1), REFINE, axis=2)
        fire_step = plan[coupling].astype(jnp.float32) * fire_delta
        level_set = jnp.where(ignition <= coupling, jnp.minimum(level_set, -1.0), level_set)
        energy = jnp.zeros_like(level_set)
        vapour = jnp.zeros_like(level_set)
        for sub_step in range(SUBSTEPS):
            padded = jnp.pad(level_set, 1, mode='edge')
            level_set, fuel_now, energy, vapour = fire_core(padded, fuel_now, energy, vapour, rate_cell, burnout, heat_cell, moist_cell, wind_fine[0], wind_fine[1], fire_step)
        flux_coarse = coarsen(jnp.stack([energy, vapour]), REFINE)
        padded_air = jnp.pad(air_field, ((0, 0), (1, 1), (1, 1), (1, 1)))
        air_field = air_core(padded_air, flux_coarse, profile)
    return (air_field, level_set, fuel_now)
```

```python
import functools
import math

import jax
import jax.numpy as jnp
from jax import lax
from jax.experimental import pallas as pl
from jax.experimental.pallas import tpu as pltpu
from jax.sharding import PartitionSpec as P

LEVELS = 80
REFINE = 10
NFUEL = 13
STEPS = 4
SUBSTEPS = 4
HALO = STEPS * SUBSTEPS
HIGH = lax.Precision.HIGHEST
MESH = pl.DeviceIdType.MESH
TINY = 1.1754944e-38
f32 = jnp.float32


def kernel(
    tiles,
    sects,
    subs,
    air_in,
    level_in,
    fuel_in,
    class_in,
    ign_in,
    plan,
    t_rate,
    t_burn,
    t_heat,
    t_moist,
    air_out,
    level_out,
    fuel_out,
    air,
    xh,
    lr,
    side,
    lv,
    bsum,
    binv,
    heat,
    moist,
    ev,
    wind,
    rx,
    ry,
    sx,
    sy,
    wsend,
    wrecv,
    hsend,
    hrecv,
    fsend,
    frecv,
    fire_s,
    fire_r,
    wind_s,
    wind_r,
    flux_s,
    flux_r,
    halo_s,
    halo_r,
):
    bands = sects * subs
    depth = air_in.shape[1]
    width = air_in.shape[3]
    rows, cols = level_in.shape
    full = rows + 2 * HALO
    lanes = cols + 128
    chunks = rows // 8
    all_chunks = full // 8
    coarse = cols // REFINE
    tile_at = lax.axis_index("tile")
    sect_at = lax.axis_index("sect")
    sub_at = lax.axis_index("sub")
    band = sect_at * subs + sub_at
    not_first = tile_at > 0
    not_final = tile_at < tiles - 1
    band_low = band > 0
    band_high = band < bands - 1

    def device(tile_step, at_band):
        return {
            "tile": tile_at + tile_step,
            "sect": at_band // subs,
            "sub": at_band % subs,
        }

    def both(a, b):
        return jnp.logical_and(a, b)

    pending = []

    def send(condition, src, dst, send_sem, recv_sem, where):
        def make():
            return pltpu.make_async_remote_copy(
                src_ref=src,
                dst_ref=dst,
                send_sem=send_sem,
                recv_sem=recv_sem,
                device_id=where,
                device_id_type=MESH,
            )

        @pl.when(condition)
        def _():
            make().start()

        pending.append((condition, make))

    def receive(condition, dst, recv_sem, send_sem, where):
        @pl.when(condition)
        def _():
            pltpu.make_async_remote_copy(
                src_ref=dst,
                dst_ref=dst,
                send_sem=send_sem,
                recv_sem=recv_sem,
                device_id=where,
                device_id_type=MESH,
            ).wait_recv()

    @pl.when(jnp.logical_not(not_first))
    def _():
        hrecv[:, 1] = jnp.zeros_like(hrecv[:, 1])
        lr[:, rows + HALO :, :cols] = jnp.zeros((3, HALO, cols), f32)

        def zero(i, carry):
            for c in range(STEPS):
                for f in range(4):
                    xh[c, 0, f, i] = jnp.zeros((8, width), f32)
            return carry

        lax.fori_loop(0, depth, zero, 0)

    @pl.when(jnp.logical_not(not_final))
    def _():
        hrecv[:, 0] = jnp.zeros_like(hrecv[:, 0])
        lr[:, rows : rows + HALO, :cols] = jnp.zeros((3, HALO, cols), f32)

        def zero(i, carry):
            for c in range(STEPS):
                for f in range(4):
                    xh[c, 1, f, i] = jnp.zeros((8, width), f32)
            return carry

        lax.fori_loop(0, depth, zero, 0)

    @pl.when(jnp.logical_not(band_low))
    def _():
        for c in range(STEPS):
            air[c, :, 0] = jnp.zeros((4, 8, width), f32)
        side[1] = jnp.zeros((3, full, 128), f32)

    @pl.when(jnp.logical_not(band_high))
    def _():
        for c in range(STEPS):
            air[c, :, depth + 1] = jnp.zeros((4, 8, width), f32)
        side[0] = jnp.zeros((3, full, 128), f32)

    @pl.when(jnp.logical_not(both(both(not_first, not_final), both(band_low, band_high))))
    def _():
        @pl.when(jnp.logical_not(not_first))
        def _():
            side[:, :, rows + HALO :] = jnp.zeros((2, 3, HALO, 128), f32)

        @pl.when(jnp.logical_not(not_final))
        def _():
            side[:, :, rows : rows + HALO] = jnp.zeros((2, 3, HALO, 128), f32)

    barrier = pltpu.get_barrier_semaphore()
    for tile_step, condition in ((0, None), (-1, not_first), (1, not_final)):
        for j in range(bands):
            ok = (band != j) if condition is None else condition

            @pl.when(ok)
            def _(tile_step=tile_step, j=j):
                pl.semaphore_signal(
                    barrier, inc=1, device_id=device(tile_step, j), device_id_type=MESH
                )

    row8 = lax.broadcasted_iota(jnp.int32, (8, width), 0)
    total_col = sum(math.exp(-k / LEVELS) for k in range(LEVELS))
    total_prof = sum(math.exp(-2.0 * k / LEVELS) for k in range(LEVELS))
    col_base = f32(0.0)
    prof_base = f32(0.0)
    for j in range(bands):
        here = band == j
        col_base = jnp.where(here, f32(math.exp(-j * depth / LEVELS) / total_col), col_base)
        prof_base = jnp.where(
            here, f32(LEVELS * math.exp(-2.0 * j * depth / LEVELS) / total_prof), prof_base
        )
    col_ratio = math.exp(-1.0 / LEVELS)
    prof_ratio = math.exp(-2.0 / LEVELS)

    def first_air(i, carry):
        weight, total_u, total_v = carry
        for f in range(4):
            air[0, f, i + 1] = air_in[f, i]
        total_u = total_u + weight * air_in[2, i]
        total_v = total_v + weight * air_in[3, i]
        return weight * f32(col_ratio), total_u, total_v

    nothing = jnp.zeros((8, width), f32)
    _, total_u, total_v = lax.fori_loop(0, depth, first_air, (col_base, nothing, nothing))

    def lookup(i, carry):
        at = pl.ds(pl.multiple_of(i * 8, 8), 8)
        kind = class_in[at, :]
        zero = jnp.zeros((8, cols), f32)
        rate, burn, hot, wet = zero, zero, zero, zero
        for k in range(NFUEL):
            same = kind == k
            rate = jnp.where(same, t_rate[k], rate)
            burn = jnp.where(same, t_burn[k], burn)
            hot = jnp.where(same, t_heat[k], hot)
            wet = jnp.where(same, t_moist[k], wet)
        lr[0, at, :cols] = level_in[at, :]
        lr[1, at, :cols] = rate
        lr[2, at, :cols] = ign_in[at, :].astype(f32)
        binv[at, :] = 1.0 / burn
        heat[at, :] = hot
        moist[at, :] = wet
        fuel_out[at, :] = fuel_in[at, :]
        return carry

    lax.fori_loop(0, chunks, lookup, 0)

    expected = (
        bands - 1 + bands * (not_first.astype(jnp.int32) + not_final.astype(jnp.int32))
    )
    pl.semaphore_wait(barrier, expected)

    def send_wind(c, total_u, total_v):
        stacked = jnp.concatenate([total_u, total_v], axis=0)
        row = lax.broadcasted_iota(jnp.int32, (8, 128), 0)
        for j in range(bands):
            shift = (128 // 4 - coarse * j) % width
            window = (pltpu.roll(stacked, shift, 1) if shift else stacked)[:, :128]
            wsend[c, j] = window
            turned = pltpu.roll(window[8:], 4, 0)
            hsend[c, 0, j] = jnp.where(row < 4, window[:8], turned)
            hsend[c, 1, j] = jnp.where(row >= 4, window[:8], turned)

            @pl.when(band == j)
            def _(window=window, j=j):
                wrecv[c, j] = window

        for j in range(bands):
            send(
                band != j,
                wsend.at[c, j],
                wrecv.at[c, band],
                wind_s.at[c, 2, j],
                wind_r.at[c, 2, band],
                device(0, j),
            )
        for way, tile_step, ok in ((0, -1, not_first), (1, 1, not_final)):
            for j in range(bands):
                send(
                    ok,
                    hsend.at[c, way, j],
                    hrecv.at[c, way, band],
                    wind_s.at[c, way, j],
                    wind_r.at[c, way, band],
                    device(tile_step, j),
                )

    def wait_wind(c):
        for j in range(bands):
            receive(band != j, wrecv.at[c, j], wind_r.at[c, 2, j], wind_s.at[c, 2, j], device(0, j))
        for way, tile_step, ok in ((0, 1, not_final), (1, -1, not_first)):
            for j in range(bands):
                receive(
                    ok,
                    hrecv.at[c, way, j],
                    wind_r.at[c, way, j],
                    wind_s.at[c, way, j],
                    device(tile_step, j),
                )

    def send_air(c):
        send(
            not_final,
            air.at[c, :, pl.ds(1, depth), pl.ds(7, 1), :],
            xh.at[c, 0, :, :, pl.ds(7, 1), :],
            halo_s.at[c, 0],
            halo_r.at[c, 0],
            device(1, band),
        )
        send(
            not_first,
            air.at[c, :, pl.ds(1, depth), pl.ds(0, 1), :],
            xh.at[c, 1, :, :, pl.ds(0, 1), :],
            halo_s.at[c, 1],
            halo_r.at[c, 1],
            device(-1, band),
        )
        send(
            band_high,
            air.at[c, :, depth],
            air.at[c, :, 0],
            halo_s.at[c, 2],
            halo_r.at[c, 2],
            device(0, band + 1),
        )
        send(
            band_low,
            air.at[c, :, 1],
            air.at[c, :, depth + 1],
            halo_s.at[c, 3],
            halo_r.at[c, 3],
            device(0, band - 1),
        )

    def wait_air(c):
        receive(
            not_first,
            xh.at[c, 0, :, :, pl.ds(7, 1), :],
            halo_r.at[c, 0],
            halo_s.at[c, 0],
            device(-1, band),
        )
        receive(
            not_final,
            xh.at[c, 1, :, :, pl.ds(0, 1), :],
            halo_r.at[c, 1],
            halo_s.at[c, 1],
            device(1, band),
        )
        receive(band_low, air.at[c, :, 0], halo_r.at[c, 2], halo_s.at[c, 2], device(0, band - 1))
        receive(
            band_high,
            air.at[c, :, depth + 1],
            halo_r.at[c, 3],
            halo_s.at[c, 3],
            device(0, band + 1),
        )

    send_wind(0, total_u, total_v)
    low_rows, high_rows = pl.ds(0, HALO), pl.ds(rows - HALO, HALO)
    own_rows = pl.ds(0, rows)
    from_next, from_last = pl.ds(rows, HALO), pl.ds(rows + HALO, HALO)
    low_cols, high_cols, own_cols = pl.ds(0, 128), pl.ds(cols - 128, 128), pl.ds(0, cols)
    index = 0
    waits = []
    for tile_step in (-1, 0, 1):
        for band_step in (-1, 0, 1):
            if tile_step == 0 and band_step == 0:
                continue
            src_rows = {-1: low_rows, 0: own_rows, 1: high_rows}[tile_step]
            dst_rows = {-1: from_next, 0: own_rows, 1: from_last}[tile_step]
            src_cols = {-1: low_cols, 0: own_cols, 1: high_cols}[band_step]
            if band_step == 0:
                dst = lr.at[:, dst_rows, own_cols]
            else:
                dst = side.at[0 if band_step < 0 else 1, :, dst_rows, :]
            tile_to = {-1: not_first, 0: None, 1: not_final}
            band_to = {-1: band_low, 0: None, 1: band_high}

            def joined(a, b):
                return b if a is None else (a if b is None else both(a, b))

            send(
                joined(tile_to[tile_step], band_to[band_step]),
                lr.at[:, src_rows, src_cols],
                dst,
                fire_s.at[index],
                fire_r.at[index],
                device(tile_step, band + band_step),
            )
            waits.append(
                (
                    joined(tile_to[-tile_step], band_to[-band_step]),
                    dst,
                    fire_r.at[index],
                    fire_s.at[index],
                    device(-tile_step, band - band_step),
                )
            )
            index += 1
    send_air(0)

    def iota(shape, dim):
        return lax.broadcasted_iota(jnp.int32, shape, dim)

    shape = (2 * full, 32)
    line, source = iota(shape, 0), iota(shape, 1)
    field = (line >= full).astype(jnp.int32)
    line = line - full * field
    own = both(
        line < rows,
        both(
            REFINE * (source - 8 * field) <= line,
            line < REFINE * (source - 8 * field) + REFINE,
        ),
    )
    after = both(
        both(line >= rows, line < rows + HALO),
        source == 16 + 4 * field + (line >= rows + REFINE).astype(jnp.int32),
    )
    before = both(
        line >= rows + HALO,
        source == 30 - 4 * field + (line >= rows + 2 * HALO - REFINE).astype(jnp.int32),
    )
    rx[...] = jnp.where(own | after | before, 1.0, 0.0)
    shape = (128, lanes)
    place, line = iota(shape, 0) - 32, iota(shape, 1)
    line = jnp.where(line < cols + 64, line, line - lanes)
    ry[...] = jnp.where(both(REFINE * place <= line, line < REFINE * place + REFINE), 1.0, 0.0)
    shape = (16, 2 * rows)
    place, line = iota(shape, 0), iota(shape, 1)
    sx[...] = jnp.where(both(REFINE * place <= line, line < REFINE * place + REFINE), 1.0, 0.0)
    shape = (cols, 128)
    line, place = iota(shape, 0), iota(shape, 1) - coarse * (band % 2)
    sy[...] = jnp.where(both(REFINE * place <= line, line < REFINE * place + REFINE), 1.0, 0.0)

    for wait in waits:
        receive(*wait)
    lane = iota((full, 128), 1)
    for k in range(3):
        lr[k, :, cols:] = jnp.where(lane < 64, side[0, k], side[1, k])
    lv[0] = lr[0]
    lv[1] = lr[0]

    row_f = iota((8, lanes), 0)
    lane_f = iota((8, lanes), 1)
    low_lane = jnp.where(band_low, -1, 0)
    high_lane = jnp.where(band_high, -1, cols - 1)

    def advance(src, i, fire_step, burn):
        at = pl.ds(pl.multiple_of(i * 8, 8), 8)
        last = pl.ds(pl.multiple_of(((i + all_chunks - 1) % all_chunks) * 8, 8), 8)
        following = pl.ds(pl.multiple_of(((i + 1) % all_chunks) * 8, 8), 8)
        here = lv[src, at, :]
        west = pltpu.roll(jnp.where(row_f == 7, lv[src, last, :], here), 1, 0)
        east = pltpu.roll(jnp.where(row_f == 0, lv[src, following, :], here), 7, 0)
        south = pltpu.roll(here, 1, 1)
        north = pltpu.roll(here, lanes - 1, 1)
        dw, de, ds, dn = here - west, east - here, here - south, north - here
        if burn:
            low_row = jnp.where(both(i == 0, jnp.logical_not(not_first)), 0, -1)
            high_row = jnp.where(both(i == chunks - 1, jnp.logical_not(not_final)), 7, -1)
            dw = jnp.where(row_f == low_row, 0.0, dw)
            de = jnp.where(row_f == high_row, 0.0, de)
        ds = jnp.where(lane_f == low_lane, 0.0, ds)
        dn = jnp.where(lane_f == high_lane, 0.0, dn)
        up_w, up_e = jnp.maximum(dw, 0.0), jnp.minimum(de, 0.0)
        up_s, up_n = jnp.maximum(ds, 0.0), jnp.minimum(dn, 0.0)
        square = (up_w * up_w + up_e * up_e) + (up_s * up_s + up_n * up_n)
        steep = square * lax.rsqrt(jnp.maximum(square, TINY))
        gx, gy = dw + de, ds + dn
        at_v = pl.ds(pl.multiple_of(full + i * 8, 8), 8)
        tail = (wind[at, :] * gx + wind[at_v, :] * gy) * lax.rsqrt(gx * gx + gy * gy + 4.0)
        speed = (fire_step * lr[1, at, :]) * (1.0 + 0.5 * jnp.maximum(tail, 0.0))
        new = here - speed * steep
        lv[1 - src, at, :] = new
        if burn:
            bsum[at, :] = bsum[at, :] + jnp.clip(0.5 - new[:, :cols], 0.0, 1.0)

    lane_a = lax.broadcasted_iota(jnp.int32, (8, width), 1)

    for c in range(STEPS):
        fire_step = plan[c].astype(f32) * f32(0.15)

        def ignite(i, carry):
            at = pl.ds(pl.multiple_of(i * 8, 8), 8)
            now = lv[0, at, :]
            lv[0, at, :] = jnp.where(lr[2, at, :] <= float(c), jnp.minimum(now, -1.0), now)
            return carry

        lax.fori_loop(0, all_chunks, ignite, 0)
        bsum[...] = jnp.zeros_like(bsum)
        wait_wind(c)
        own = wrecv[c, 0]
        after = hrecv[c, 0, 0]
        before = hrecv[c, 1, 0]
        for j in range(1, bands):
            own = own + wrecv[c, j]
            after = after + hrecv[c, 0, j]
            before = before + hrecv[c, 1, j]
        together = jnp.concatenate([own, after, before], axis=0)
        wide = jnp.dot(together, ry[...], precision=HIGH, preferred_element_type=f32)
        wind[...] = jnp.dot(rx[...], wide, precision=HIGH, preferred_element_type=f32)

        near = (SUBSTEPS * (STEPS - c)) > 8

        def pair(k, carry):
            for src in (0, 1):

                def inner(i, carry):
                    advance(src, i, fire_step, True)
                    return carry

                lax.fori_loop(0, chunks, inner, 0)
                if near:

                    def outer(i, carry):
                        advance(src, i, fire_step, False)
                        return carry

                    lax.fori_loop(chunks, all_chunks, outer, 0)
                else:
                    advance(src, chunks, fire_step, False)
                    advance(src, all_chunks - 1, fire_step, False)
            return carry

        lax.fori_loop(0, SUBSTEPS // 2, pair, 0)

        def burn(i, carry):
            at = pl.ds(pl.multiple_of(i * 8, 8), 8)
            fuel = fuel_out[at, :]
            remain = fuel * jnp.exp(-fire_step * bsum[at, :] * binv[at, :])
            used = fuel - remain
            fuel_out[at, :] = remain
            ev[at, :] = used * heat[at, :]
            ev[pl.ds(pl.multiple_of(rows + i * 8, 8), 8), :] = used * moist[at, :]
            return carry

        lax.fori_loop(0, chunks, burn, 0)
        lines = jnp.dot(sx[...], ev[...], precision=HIGH, preferred_element_type=f32)
        flux = jnp.dot(lines, sy[...], precision=HIGH, preferred_element_type=f32)
        flux = flux * f32(1.0 / (REFINE * REFINE))
        fsend[c] = flux
        for j in range(bands):

            @pl.when(band == j)
            def _(j=j):
                frecv[c, j] = flux

            send(
                band != j,
                fsend.at[c],
                frecv.at[c, band],
                flux_s.at[c, j],
                flux_r.at[c, band],
                device(0, j),
            )

        wait_air(c)
        final = c == STEPS - 1

        def write(f, i, value):
            if final:
                air_out[f, i] = value
            else:
                air[c + 1, f, i + 1] = value

        def update(i, carry):
            weight, total_u, total_v = carry
            u, v = air[c, 2, i + 1], air[c, 3, i + 1]
            u_up, u_dn = jnp.maximum(u, 0.0), jnp.minimum(u, 0.0)
            v_up, v_dn = jnp.maximum(v, 0.0), jnp.minimum(v, 0.0)
            lift_x = lift_y = None
            for f in range(4):
                here = air[c, f, i + 1]
                west = pltpu.roll(jnp.where(row8 == 7, xh[c, 0, f, i], here), 1, 0)
                east = pltpu.roll(jnp.where(row8 == 0, xh[c, 1, f, i], here), 7, 0)
                south = jnp.where(lane_a == 0, 0.0, pltpu.roll(here, 1, 1))
                north = jnp.where(lane_a == width - 1, 0.0, pltpu.roll(here, width - 1, 1))
                dw, de, ds, dn = here - west, east - here, here - south, north - here
                advect = u_up * dw + u_dn * de + v_up * ds + v_dn * dn
                lap = (de - dw) + (dn - ds) + (
                    (air[c, f, i] + air[c, f, i + 2]) - 2.0 * here
                )
                new = here + 0.1 * (0.2 * lap - advect)
                if f == 0:
                    lift_x, lift_y = east - west, north - south
                elif f == 1:
                    lift_x = lift_x + 0.6 * (east - west)
                    lift_y = lift_y + 0.6 * (north - south)
                elif f == 2:
                    new = new + 0.015 * lift_x
                    total_u = total_u + weight * new
                else:
                    new = new + 0.015 * lift_y
                    total_v = total_v + weight * new
                write(f, i, new)
            return weight * f32(col_ratio), total_u, total_v

        _, total_u, total_v = lax.fori_loop(0, depth, update, (col_base, nothing, nothing))
        if not final:
            send_wind(c + 1, total_u, total_v)
        for j in range(bands):
            receive(band != j, frecv.at[c, j], flux_r.at[c, j], flux_s.at[c, j], device(0, j))
        parts = [
            frecv[c, 2 * k] + frecv[c, 2 * k + 1] for k in range(width // 128)
        ]
        whole = jnp.concatenate(parts, axis=1)
        heat_in, moist_in = whole[:8], whole[8:]

        def force(i, weight):
            for f, flux in ((0, heat_in), (1, moist_in)):
                now = air_out[f, i] if final else air[c + 1, f, i + 1]
                write(f, i, now + weight * flux)
            return weight * f32(prof_ratio)

        lax.fori_loop(0, depth, force, prof_base * f32(2.0))
        if not final:
            send_air(c + 1)

    level_out[...] = lv[0, :rows, :cols]
    for condition, make in pending:

        @pl.when(condition)
        def _(make=make):
            make().wait_send()


def solution(mesh):
    tiles, sects, subs = (mesh.shape[name] for name in ("tile", "sect", "sub"))
    bands = sects * subs
    air_spec = P(None, ("sect", "sub"), ("group", "tile"), None)
    fire_spec = P(("group", "tile"), ("sect", "sub"))

    def local(air_state, fire_level, *rest):
        depth, width = air_state.shape[1], air_state.shape[3]
        rows, cols = fire_level.shape
        full, lanes = rows + 2 * HALO, cols + 128
        assert air_state.shape[2] == 8 and cols == 64 * REFINE and rows == 8 * REFINE
        vmem = pl.BlockSpec(memory_space=pltpu.VMEM)
        smem = pl.BlockSpec(memory_space=pltpu.SMEM)
        dma = pltpu.SemaphoreType.DMA
        return pl.pallas_call(
            functools.partial(kernel, tiles, sects, subs),
            out_shape=(
                jax.ShapeDtypeStruct(air_state.shape, f32),
                jax.ShapeDtypeStruct(fire_level.shape, f32),
                jax.ShapeDtypeStruct(fire_level.shape, f32),
            ),
            in_specs=[vmem] * 5 + [smem] * 5,
            out_specs=(vmem, vmem, vmem),
            scratch_shapes=[
                pltpu.VMEM((STEPS, 4, depth + 2, 8, width), f32),
                pltpu.VMEM((STEPS, 2, 4, depth, 8, width), f32),
                pltpu.VMEM((3, full, lanes), f32),
                pltpu.VMEM((2, 3, full, 128), f32),
                pltpu.VMEM((2, full, lanes), f32),
                pltpu.VMEM((rows, cols), f32),
                pltpu.VMEM((rows, cols), f32),
                pltpu.VMEM((rows, cols), f32),
                pltpu.VMEM((rows, cols), f32),
                pltpu.VMEM((2 * rows, cols), f32),
                pltpu.VMEM((2 * full, lanes), f32),
                pltpu.VMEM((2 * full, 32), f32),
                pltpu.VMEM((128, lanes), f32),
                pltpu.VMEM((16, 2 * rows), f32),
                pltpu.VMEM((cols, 128), f32),
                pltpu.VMEM((STEPS, bands, 16, 128), f32),
                pltpu.VMEM((STEPS, bands, 16, 128), f32),
                pltpu.VMEM((STEPS, 2, bands, 8, 128), f32),
                pltpu.VMEM((STEPS, 2, bands, 8, 128), f32),
                pltpu.VMEM((STEPS, 16, 128), f32),
                pltpu.VMEM((STEPS, bands, 16, 128), f32),
                dma((8,)),
                dma((8,)),
                dma((STEPS, 3, bands)),
                dma((STEPS, 3, bands)),
                dma((STEPS, bands)),
                dma((STEPS, bands)),
                dma((STEPS, 4)),
                dma((STEPS, 4)),
            ],
            compiler_params=pltpu.CompilerParams(
                collective_id=0, has_side_effects=True, vmem_limit_bytes=56 * 1024 * 1024
            ),
        )(air_state, fire_level, *rest)

    return jax.shard_map(
        local,
        mesh=mesh,
        in_specs=(air_spec, fire_spec, fire_spec, fire_spec, fire_spec) + (P(),) * 5,
        out_specs=(air_spec, fire_spec, fire_spec),
        check_vma=False,
    )
```

```python
import functools
import math

import jax
import jax.numpy as jnp
from jax import lax
from jax.experimental import pallas as pl
from jax.experimental.pallas import tpu as pltpu
from jax.sharding import PartitionSpec as P

LEVELS = 80
REFINE = 10
NFUEL = 13
STEPS = 4
SUBSTEPS = 4
HALO = STEPS * SUBSTEPS
MESH = pl.DeviceIdType.MESH
TINY = 1.1754944e-38
f32 = jnp.float32
bf16 = jnp.bfloat16


def split(value, axis, pieces):
    parts = []
    for _ in range(pieces):
        parts.append(value.astype(bf16))
        value = value - parts[-1].astype(f32)
    return jnp.concatenate(parts, axis=axis)


def repeated(mask, axis, pieces):
    return jnp.concatenate([jnp.where(mask, 1.0, 0.0).astype(bf16)] * pieces, axis=axis)


def kernel(
    tiles,
    sects,
    subs,
    air_in,
    level_in,
    fuel_in,
    class_in,
    ign_in,
    plan,
    t_rate,
    t_burn,
    t_heat,
    t_moist,
    air_out,
    level_out,
    fuel_out,
    air,
    xh,
    lr,
    side,
    lv,
    bsum,
    binv,
    heat,
    moist,
    ev,
    wind,
    rx,
    ry,
    sx,
    sy,
    wsend,
    wrecv,
    hsend,
    hrecv,
    fsend,
    frecv,
    fire_s,
    fire_r,
    wind_s,
    wind_r,
    flux_s,
    flux_r,
    halo_s,
    halo_r,
):
    bands = sects * subs
    depth = air_in.shape[1]
    width = air_in.shape[3]
    rows, cols = level_in.shape
    full = rows + 2 * HALO
    lanes = cols + 128
    chunks = rows // 8
    all_chunks = full // 8
    coarse = cols // REFINE
    tile_at = lax.axis_index("tile")
    sect_at = lax.axis_index("sect")
    sub_at = lax.axis_index("sub")
    band = sect_at * subs + sub_at
    not_first = tile_at > 0
    not_final = tile_at < tiles - 1
    band_low = band > 0
    band_high = band < bands - 1

    def device(tile_step, at_band):
        return {
            "tile": tile_at + tile_step,
            "sect": at_band // subs,
            "sub": at_band % subs,
        }

    def both(a, b):
        return jnp.logical_and(a, b)

    pending = []

    def send(condition, src, dst, send_sem, recv_sem, where):
        def make():
            return pltpu.make_async_remote_copy(
                src_ref=src,
                dst_ref=dst,
                send_sem=send_sem,
                recv_sem=recv_sem,
                device_id=where,
                device_id_type=MESH,
            )

        @pl.when(condition)
        def _():
            make().start()

        pending.append((condition, make))

    def receive(condition, dst, recv_sem, send_sem, where):
        @pl.when(condition)
        def _():
            pltpu.make_async_remote_copy(
                src_ref=dst,
                dst_ref=dst,
                send_sem=send_sem,
                recv_sem=recv_sem,
                device_id=where,
                device_id_type=MESH,
            ).wait_recv()

    @pl.when(jnp.logical_not(not_first))
    def _():
        hrecv[:, 1] = jnp.zeros_like(hrecv[:, 1])
        lr[:, rows + HALO :, :cols] = jnp.zeros((3, HALO, cols), f32)

        def zero(i, carry):
            for c in range(STEPS):
                for f in range(4):
                    xh[c, 0, f, i] = jnp.zeros((8, width), f32)
            return carry

        lax.fori_loop(0, depth, zero, 0)

    @pl.when(jnp.logical_not(not_final))
    def _():
        hrecv[:, 0] = jnp.zeros_like(hrecv[:, 0])
        lr[:, rows : rows + HALO, :cols] = jnp.zeros((3, HALO, cols), f32)

        def zero(i, carry):
            for c in range(STEPS):
                for f in range(4):
                    xh[c, 1, f, i] = jnp.zeros((8, width), f32)
            return carry

        lax.fori_loop(0, depth, zero, 0)

    @pl.when(jnp.logical_not(band_low))
    def _():
        for c in range(STEPS):
            air[c, :, 0] = jnp.zeros((4, 8, width), f32)
        side[1] = jnp.zeros((3, full, 128), f32)

    @pl.when(jnp.logical_not(band_high))
    def _():
        for c in range(STEPS):
            air[c, :, depth + 1] = jnp.zeros((4, 8, width), f32)
        side[0] = jnp.zeros((3, full, 128), f32)

    @pl.when(jnp.logical_not(both(both(not_first, not_final), both(band_low, band_high))))
    def _():
        @pl.when(jnp.logical_not(not_first))
        def _():
            side[:, :, rows + HALO :] = jnp.zeros((2, 3, HALO, 128), f32)

        @pl.when(jnp.logical_not(not_final))
        def _():
            side[:, :, rows : rows + HALO] = jnp.zeros((2, 3, HALO, 128), f32)

    barrier = pltpu.get_barrier_semaphore()
    for tile_step, condition in ((0, None), (-1, not_first), (1, not_final)):
        for j in range(bands):
            ok = (band != j) if condition is None else condition

            @pl.when(ok)
            def _(tile_step=tile_step, j=j):
                pl.semaphore_signal(
                    barrier, inc=1, device_id=device(tile_step, j), device_id_type=MESH
                )

    row8 = lax.broadcasted_iota(jnp.int32, (8, width), 0)
    total_col = sum(math.exp(-k / LEVELS) for k in range(LEVELS))
    total_prof = sum(math.exp(-2.0 * k / LEVELS) for k in range(LEVELS))
    col_base = f32(0.0)
    prof_base = f32(0.0)
    for j in range(bands):
        here = band == j
        col_base = jnp.where(here, f32(math.exp(-j * depth / LEVELS) / total_col), col_base)
        prof_base = jnp.where(
            here, f32(LEVELS * math.exp(-2.0 * j * depth / LEVELS) / total_prof), prof_base
        )
    col_ratio = math.exp(-1.0 / LEVELS)
    prof_ratio = math.exp(-2.0 / LEVELS)

    def first_air(i, carry):
        weight, total_u, total_v = carry
        for f in range(4):
            air[0, f, i + 1] = air_in[f, i]
        total_u = total_u + weight * air_in[2, i]
        total_v = total_v + weight * air_in[3, i]
        return weight * f32(col_ratio), total_u, total_v

    nothing = jnp.zeros((8, width), f32)
    _, total_u, total_v = lax.fori_loop(0, depth, first_air, (col_base, nothing, nothing))

    def lookup(i, carry):
        at = pl.ds(pl.multiple_of(i * 8, 8), 8)
        kind = class_in[at, :]
        zero = jnp.zeros((8, cols), f32)
        rate, burn, hot, wet = zero, zero, zero, zero
        for k in range(NFUEL):
            same = kind == k
            rate = jnp.where(same, t_rate[k], rate)
            burn = jnp.where(same, t_burn[k], burn)
            hot = jnp.where(same, t_heat[k], hot)
            wet = jnp.where(same, t_moist[k], wet)
        lr[0, at, :cols] = level_in[at, :]
        lr[1, at, :cols] = rate
        lr[2, at, :cols] = ign_in[at, :].astype(f32)
        binv[at, :] = 1.0 / burn
        heat[at, :] = hot
        moist[at, :] = wet
        fuel_out[at, :] = fuel_in[at, :]
        return carry

    lax.fori_loop(0, chunks, lookup, 0)

    expected = (
        bands - 1 + bands * (not_first.astype(jnp.int32) + not_final.astype(jnp.int32))
    )
    pl.semaphore_wait(barrier, expected)

    def send_wind(c, total_u, total_v):
        stacked = jnp.concatenate([total_u, total_v], axis=0)
        row = lax.broadcasted_iota(jnp.int32, (8, 128), 0)
        for j in range(bands):
            shift = (128 // 4 - coarse * j) % width
            window = (pltpu.roll(stacked, shift, 1) if shift else stacked)[:, :128]
            wsend[c, j] = window
            turned = pltpu.roll(window[8:], 4, 0)
            hsend[c, 0, j] = jnp.where(row < 4, window[:8], turned)
            hsend[c, 1, j] = jnp.where(row >= 4, window[:8], turned)

            @pl.when(band == j)
            def _(window=window, j=j):
                wrecv[c, j] = window

        for j in range(bands):
            send(
                band != j,
                wsend.at[c, j],
                wrecv.at[c, band],
                wind_s.at[c, 2, j],
                wind_r.at[c, 2, band],
                device(0, j),
            )
        for way, tile_step, ok in ((0, -1, not_first), (1, 1, not_final)):
            for j in range(bands):
                send(
                    ok,
                    hsend.at[c, way, j],
                    hrecv.at[c, way, band],
                    wind_s.at[c, way, j],
                    wind_r.at[c, way, band],
                    device(tile_step, j),
                )

    def wait_wind(c):
        for j in range(bands):
            receive(band != j, wrecv.at[c, j], wind_r.at[c, 2, j], wind_s.at[c, 2, j], device(0, j))
        for way, tile_step, ok in ((0, 1, not_final), (1, -1, not_first)):
            for j in range(bands):
                receive(
                    ok,
                    hrecv.at[c, way, j],
                    wind_r.at[c, way, j],
                    wind_s.at[c, way, j],
                    device(tile_step, j),
                )

    def send_air(c):
        send(
            not_final,
            air.at[c, :, pl.ds(1, depth), pl.ds(7, 1), :],
            xh.at[c, 0, :, :, pl.ds(7, 1), :],
            halo_s.at[c, 0],
            halo_r.at[c, 0],
            device(1, band),
        )
        send(
            not_first,
            air.at[c, :, pl.ds(1, depth), pl.ds(0, 1), :],
            xh.at[c, 1, :, :, pl.ds(0, 1), :],
            halo_s.at[c, 1],
            halo_r.at[c, 1],
            device(-1, band),
        )
        send(
            band_high,
            air.at[c, :, depth],
            air.at[c, :, 0],
            halo_s.at[c, 2],
            halo_r.at[c, 2],
            device(0, band + 1),
        )
        send(
            band_low,
            air.at[c, :, 1],
            air.at[c, :, depth + 1],
            halo_s.at[c, 3],
            halo_r.at[c, 3],
            device(0, band - 1),
        )

    def wait_air(c):
        receive(
            not_first,
            xh.at[c, 0, :, :, pl.ds(7, 1), :],
            halo_r.at[c, 0],
            halo_s.at[c, 0],
            device(-1, band),
        )
        receive(
            not_final,
            xh.at[c, 1, :, :, pl.ds(0, 1), :],
            halo_r.at[c, 1],
            halo_s.at[c, 1],
            device(1, band),
        )
        receive(band_low, air.at[c, :, 0], halo_r.at[c, 2], halo_s.at[c, 2], device(0, band - 1))
        receive(
            band_high,
            air.at[c, :, depth + 1],
            halo_r.at[c, 3],
            halo_s.at[c, 3],
            device(0, band + 1),
        )

    send_wind(0, total_u, total_v)
    low_rows, high_rows = pl.ds(0, HALO), pl.ds(rows - HALO, HALO)
    own_rows = pl.ds(0, rows)
    from_next, from_last = pl.ds(rows, HALO), pl.ds(rows + HALO, HALO)
    low_cols, high_cols, own_cols = pl.ds(0, 128), pl.ds(cols - 128, 128), pl.ds(0, cols)
    index = 0
    waits = []
    for tile_step in (-1, 0, 1):
        for band_step in (-1, 0, 1):
            if tile_step == 0 and band_step == 0:
                continue
            src_rows = {-1: low_rows, 0: own_rows, 1: high_rows}[tile_step]
            dst_rows = {-1: from_next, 0: own_rows, 1: from_last}[tile_step]
            src_cols = {-1: low_cols, 0: own_cols, 1: high_cols}[band_step]
            if band_step == 0:
                dst = lr.at[:, dst_rows, own_cols]
            else:
                dst = side.at[0 if band_step < 0 else 1, :, dst_rows, :]
            tile_to = {-1: not_first, 0: None, 1: not_final}
            band_to = {-1: band_low, 0: None, 1: band_high}

            def joined(a, b):
                return b if a is None else (a if b is None else both(a, b))

            send(
                joined(tile_to[tile_step], band_to[band_step]),
                lr.at[:, src_rows, src_cols],
                dst,
                fire_s.at[index],
                fire_r.at[index],
                device(tile_step, band + band_step),
            )
            waits.append(
                (
                    joined(tile_to[-tile_step], band_to[-band_step]),
                    dst,
                    fire_r.at[index],
                    fire_s.at[index],
                    device(-tile_step, band - band_step),
                )
            )
            index += 1
    send_air(0)

    def iota(shape, dim):
        return lax.broadcasted_iota(jnp.int32, shape, dim)

    shape = (2 * full, 32)
    line, source = iota(shape, 0), iota(shape, 1)
    field = (line >= full).astype(jnp.int32)
    line = line - full * field
    own = both(
        line < rows,
        both(
            REFINE * (source - 8 * field) <= line,
            line < REFINE * (source - 8 * field) + REFINE,
        ),
    )
    after = both(
        both(line >= rows, line < rows + HALO),
        source == 16 + 4 * field + (line >= rows + REFINE).astype(jnp.int32),
    )
    before = both(
        line >= rows + HALO,
        source == 30 - 4 * field + (line >= rows + 2 * HALO - REFINE).astype(jnp.int32),
    )
    rx[...] = repeated(own | after | before, 1, 3)
    shape = (128, lanes)
    place, line = iota(shape, 0) - 32, iota(shape, 1)
    line = jnp.where(line < cols + 64, line, line - lanes)
    ry[...] = repeated(both(REFINE * place <= line, line < REFINE * place + REFINE), 0, 2)
    shape = (16, 2 * rows)
    place, line = iota(shape, 0), iota(shape, 1)
    sx[...] = repeated(both(REFINE * place <= line, line < REFINE * place + REFINE), 1, 3)
    shape = (cols, 128)
    line, place = iota(shape, 0), iota(shape, 1) - coarse * (band % 2)
    sy[...] = repeated(both(REFINE * place <= line, line < REFINE * place + REFINE), 0, 2)

    for wait in waits:
        receive(*wait)
    lane = iota((full, 128), 1)
    for k in range(3):
        lr[k, :, cols:] = jnp.where(lane < 64, side[0, k], side[1, k])
    lv[0] = lr[0]
    lv[1] = lr[0]

    row_f = iota((8, lanes), 0)
    lane_f = iota((8, lanes), 1)
    low_lane = jnp.where(band_low, -1, 0)
    high_lane = jnp.where(band_high, -1, cols - 1)

    def advance(src, i, fire_step, burn):
        at = pl.ds(pl.multiple_of(i * 8, 8), 8)
        last = pl.ds(pl.multiple_of(((i + all_chunks - 1) % all_chunks) * 8, 8), 8)
        following = pl.ds(pl.multiple_of(((i + 1) % all_chunks) * 8, 8), 8)
        here = lv[src, at, :]
        west = pltpu.roll(jnp.where(row_f == 7, lv[src, last, :], here), 1, 0)
        east = pltpu.roll(jnp.where(row_f == 0, lv[src, following, :], here), 7, 0)
        south = pltpu.roll(here, 1, 1)
        north = pltpu.roll(here, lanes - 1, 1)
        dw, de, ds, dn = here - west, east - here, here - south, north - here
        if burn:
            low_row = jnp.where(both(i == 0, jnp.logical_not(not_first)), 0, -1)
            high_row = jnp.where(both(i == chunks - 1, jnp.logical_not(not_final)), 7, -1)
            dw = jnp.where(row_f == low_row, 0.0, dw)
            de = jnp.where(row_f == high_row, 0.0, de)
        ds = jnp.where(lane_f == low_lane, 0.0, ds)
        dn = jnp.where(lane_f == high_lane, 0.0, dn)
        up_w, up_e = jnp.maximum(dw, 0.0), jnp.minimum(de, 0.0)
        up_s, up_n = jnp.maximum(ds, 0.0), jnp.minimum(dn, 0.0)
        square = (up_w * up_w + up_e * up_e) + (up_s * up_s + up_n * up_n)
        steep = square * lax.rsqrt(jnp.maximum(square, TINY))
        gx, gy = dw + de, ds + dn
        at_v = pl.ds(pl.multiple_of(full + i * 8, 8), 8)
        tail = (wind[at, :] * gx + wind[at_v, :] * gy) * lax.rsqrt(gx * gx + gy * gy + 4.0)
        speed = (fire_step * lr[1, at, :]) * (1.0 + 0.5 * jnp.maximum(tail, 0.0))
        new = here - speed * steep
        lv[1 - src, at, :] = new
        if burn:
            bsum[at, :] = bsum[at, :] + jnp.clip(0.5 - new[:, :cols], 0.0, 1.0)

    lane_a = lax.broadcasted_iota(jnp.int32, (8, width), 1)

    def write(c, f, i, value):
        if c == STEPS - 1:
            air_out[f, i] = value
        else:
            air[c + 1, f, i + 1] = value

    def move_air(c):
        wait_air(c)
        final = c == STEPS - 1

        def update(i, carry):
            weight, total_u, total_v = carry
            u, v = air[c, 2, i + 1], air[c, 3, i + 1]
            u_up, u_dn = jnp.maximum(u, 0.0), jnp.minimum(u, 0.0)
            v_up, v_dn = jnp.maximum(v, 0.0), jnp.minimum(v, 0.0)
            lift_x = lift_y = None
            for f in range(4):
                here = air[c, f, i + 1]
                west = pltpu.roll(jnp.where(row8 == 7, xh[c, 0, f, i], here), 1, 0)
                east = pltpu.roll(jnp.where(row8 == 0, xh[c, 1, f, i], here), 7, 0)
                south = jnp.where(lane_a == 0, 0.0, pltpu.roll(here, 1, 1))
                north = jnp.where(lane_a == width - 1, 0.0, pltpu.roll(here, width - 1, 1))
                dw, de, ds, dn = here - west, east - here, here - south, north - here
                advect = u_up * dw + u_dn * de + v_up * ds + v_dn * dn
                lap = (de - dw) + (dn - ds) + (
                    (air[c, f, i] + air[c, f, i + 2]) - 2.0 * here
                )
                new = here + 0.1 * (0.2 * lap - advect)
                if f == 0:
                    lift_x, lift_y = east - west, north - south
                elif f == 1:
                    lift_x = lift_x + 0.6 * (east - west)
                    lift_y = lift_y + 0.6 * (north - south)
                elif f == 2:
                    new = new + 0.015 * lift_x
                    total_u = total_u + weight * new
                else:
                    new = new + 0.015 * lift_y
                    total_v = total_v + weight * new
                write(c, f, i, new)
            return weight * f32(col_ratio), total_u, total_v

        _, total_u, total_v = lax.fori_loop(0, depth, update, (col_base, nothing, nothing), unroll=2)
        if not final:
            send_wind(c + 1, total_u, total_v)

    def finish_air(c):
        final = c == STEPS - 1
        for j in range(bands):
            receive(band != j, frecv.at[c, j], flux_r.at[c, j], flux_s.at[c, j], device(0, j))
        parts = [
            frecv[c, 2 * k] + frecv[c, 2 * k + 1] for k in range(width // 128)
        ]
        whole = jnp.concatenate(parts, axis=1)
        heat_in, moist_in = whole[:8], whole[8:]

        def force(i, weight):
            for f, flux in ((0, heat_in), (1, moist_in)):
                now = air_out[f, i] if final else air[c + 1, f, i + 1]
                write(c, f, i, now + weight * flux)
            return weight * f32(prof_ratio)

        lax.fori_loop(0, depth, force, prof_base * f32(2.0), unroll=2)

    for c in range(STEPS):
        fire_step = plan[c].astype(f32) * f32(0.15)

        def ignite(i, carry):
            at = pl.ds(pl.multiple_of(i * 8, 8), 8)
            now = lv[0, at, :]
            lv[0, at, :] = jnp.where(lr[2, at, :] <= float(c), jnp.minimum(now, -1.0), now)
            return carry

        lax.fori_loop(0, all_chunks, ignite, 0)
        bsum[...] = jnp.zeros_like(bsum)
        wait_wind(c)
        own = wrecv[c, 0]
        after = hrecv[c, 0, 0]
        before = hrecv[c, 1, 0]
        for j in range(1, bands):
            own = own + wrecv[c, j]
            after = after + hrecv[c, 0, j]
            before = before + hrecv[c, 1, j]
        together = jnp.concatenate([own, after, before], axis=0)
        wide = jnp.dot(split(together, 1, 2), ry[...], preferred_element_type=f32)
        wind[...] = jnp.dot(rx[...], split(wide, 0, 3), preferred_element_type=f32)

        near = (SUBSTEPS * (STEPS - c)) > 8

        def substep(src, fire_step=fire_step, near=near):
            def inner(i, carry):
                advance(src, i, fire_step, True)
                return carry

            lax.fori_loop(0, chunks, inner, 0, unroll=5)
            if near:

                def outer(i, carry):
                    advance(src, i, fire_step, False)
                    return carry

                lax.fori_loop(chunks, all_chunks, outer, 0, unroll=2)
            else:
                advance(src, chunks, fire_step, False)
                advance(src, all_chunks - 1, fire_step, False)

        substep(0)
        if c > 0:
            finish_air(c - 1)
            send_air(c)
        substep(1)
        substep(0)
        move_air(c)
        substep(1)

        def burn(i, carry):
            at = pl.ds(pl.multiple_of(i * 8, 8), 8)
            fuel = fuel_out[at, :]
            remain = fuel * jnp.exp(-fire_step * bsum[at, :] * binv[at, :])
            used = fuel - remain
            fuel_out[at, :] = remain
            ev[at, :] = used * heat[at, :]
            ev[pl.ds(pl.multiple_of(rows + i * 8, 8), 8), :] = used * moist[at, :]
            return carry

        lax.fori_loop(0, chunks, burn, 0)
        lines = jnp.dot(split(ev[...], 1, 2), sy[...], preferred_element_type=f32)
        flux = jnp.dot(sx[...], split(lines, 0, 3), preferred_element_type=f32)
        flux = flux * f32(1.0 / (REFINE * REFINE))
        fsend[c] = flux
        for j in range(bands):

            @pl.when(band == j)
            def _(j=j):
                frecv[c, j] = flux

            send(
                band != j,
                fsend.at[c],
                frecv.at[c, band],
                flux_s.at[c, j],
                flux_r.at[c, band],
                device(0, j),
            )

    finish_air(STEPS - 1)
    level_out[...] = lv[0, :rows, :cols]
    for condition, make in pending:

        @pl.when(condition)
        def _(make=make):
            make().wait_send()


def solution(mesh):
    tiles, sects, subs = (mesh.shape[name] for name in ("tile", "sect", "sub"))
    bands = sects * subs
    air_spec = P(None, ("sect", "sub"), ("group", "tile"), None)
    fire_spec = P(("group", "tile"), ("sect", "sub"))

    def local(air_state, fire_level, *rest):
        depth, width = air_state.shape[1], air_state.shape[3]
        rows, cols = fire_level.shape
        full, lanes = rows + 2 * HALO, cols + 128
        assert air_state.shape[2] == 8 and cols == 64 * REFINE and rows == 8 * REFINE
        vmem = pl.BlockSpec(memory_space=pltpu.VMEM)
        smem = pl.BlockSpec(memory_space=pltpu.SMEM)
        dma = pltpu.SemaphoreType.DMA
        return pl.pallas_call(
            functools.partial(kernel, tiles, sects, subs),
            out_shape=(
                jax.ShapeDtypeStruct(air_state.shape, f32),
                jax.ShapeDtypeStruct(fire_level.shape, f32),
                jax.ShapeDtypeStruct(fire_level.shape, f32),
            ),
            in_specs=[vmem] * 5 + [smem] * 5,
            out_specs=(vmem, vmem, vmem),
            scratch_shapes=[
                pltpu.VMEM((STEPS, 4, depth + 2, 8, width), f32),
                pltpu.VMEM((STEPS, 2, 4, depth, 8, width), f32),
                pltpu.VMEM((3, full, lanes), f32),
                pltpu.VMEM((2, 3, full, 128), f32),
                pltpu.VMEM((2, full, lanes), f32),
                pltpu.VMEM((rows, cols), f32),
                pltpu.VMEM((rows, cols), f32),
                pltpu.VMEM((rows, cols), f32),
                pltpu.VMEM((rows, cols), f32),
                pltpu.VMEM((2 * rows, cols), f32),
                pltpu.VMEM((2 * full, lanes), f32),
                pltpu.VMEM((2 * full, 96), bf16),
                pltpu.VMEM((256, lanes), bf16),
                pltpu.VMEM((16, 6 * rows), bf16),
                pltpu.VMEM((2 * cols, 128), bf16),
                pltpu.VMEM((STEPS, bands, 16, 128), f32),
                pltpu.VMEM((STEPS, bands, 16, 128), f32),
                pltpu.VMEM((STEPS, 2, bands, 8, 128), f32),
                pltpu.VMEM((STEPS, 2, bands, 8, 128), f32),
                pltpu.VMEM((STEPS, 16, 128), f32),
                pltpu.VMEM((STEPS, bands, 16, 128), f32),
                dma((8,)),
                dma((8,)),
                dma((STEPS, 3, bands)),
                dma((STEPS, 3, bands)),
                dma((STEPS, bands)),
                dma((STEPS, bands)),
                dma((STEPS, 4)),
                dma((STEPS, 4)),
            ],
            compiler_params=pltpu.CompilerParams(
                collective_id=0, has_side_effects=True, vmem_limit_bytes=56 * 1024 * 1024
            ),
        )(air_state, fire_level, *rest)

    return jax.shard_map(
        local,
        mesh=mesh,
        in_specs=(air_spec, fire_spec, fire_spec, fire_spec, fire_spec) + (P(),) * 5,
        out_specs=(air_spec, fire_spec, fire_spec),
        check_vma=False,
    )
```

```python
import functools
import math

import jax
import jax.numpy as jnp
from jax import lax
from jax.experimental import pallas as pl
from jax.experimental.pallas import tpu as pltpu
from jax.sharding import PartitionSpec as P

LEVELS = 80
REFINE = 10
NFUEL = 13
STEPS = 4
SUBSTEPS = 4
HALO = STEPS * SUBSTEPS
MESH = pl.DeviceIdType.MESH
TINY = 1.1754944e-38
f32 = jnp.float32
bf16 = jnp.bfloat16


def split(value, axis, pieces):
    parts = []
    for _ in range(pieces):
        parts.append(value.astype(bf16))
        value = value - parts[-1].astype(f32)
    return jnp.concatenate(parts, axis=axis)


def repeated(mask, axis, pieces):
    return jnp.concatenate([jnp.where(mask, 1.0, 0.0).astype(bf16)] * pieces, axis=axis)


def kernel(
    tiles,
    sects,
    subs,
    air_in,
    level_in,
    fuel_in,
    class_in,
    ign_in,
    plan,
    t_rate,
    t_burn,
    t_heat,
    t_moist,
    air_out,
    level_out,
    fuel_out,
    air,
    xh,
    lr,
    side,
    lv,
    bsum,
    binv,
    heat,
    moist,
    ev,
    wind,
    rx,
    ry,
    sx,
    sy,
    wsend,
    wrecv,
    hsend,
    hrecv,
    fsend,
    frecv,
    fire_s,
    fire_r,
    wind_s,
    wind_r,
    flux_s,
    flux_r,
    halo_s,
    halo_r,
):
    bands = sects * subs
    depth = air_in.shape[1]
    width = air_in.shape[3]
    rows, cols = level_in.shape
    full = rows + 2 * HALO
    lanes = cols + 128
    chunks = rows // 8
    all_chunks = full // 8
    coarse = cols // REFINE
    tile_at = lax.axis_index("tile")
    sect_at = lax.axis_index("sect")
    sub_at = lax.axis_index("sub")
    band = sect_at * subs + sub_at
    not_first = tile_at > 0
    not_final = tile_at < tiles - 1
    band_low = band > 0
    band_high = band < bands - 1

    def device(tile_step, at_band):
        return {
            "tile": tile_at + tile_step,
            "sect": at_band // subs,
            "sub": at_band % subs,
        }

    def both(a, b):
        return jnp.logical_and(a, b)

    pending = []

    def send(condition, src, dst, send_sem, recv_sem, where):
        def make():
            return pltpu.make_async_remote_copy(
                src_ref=src,
                dst_ref=dst,
                send_sem=send_sem,
                recv_sem=recv_sem,
                device_id=where,
                device_id_type=MESH,
            )

        @pl.when(condition)
        def _():
            make().start()

        pending.append((condition, make))

    def receive(condition, dst, recv_sem, send_sem, where):
        @pl.when(condition)
        def _():
            pltpu.make_async_remote_copy(
                src_ref=dst,
                dst_ref=dst,
                send_sem=send_sem,
                recv_sem=recv_sem,
                device_id=where,
                device_id_type=MESH,
            ).wait_recv()

    @pl.when(jnp.logical_not(not_first))
    def _():
        hrecv[:, 1] = jnp.zeros_like(hrecv[:, 1])
        lr[:, rows + HALO :, :cols] = jnp.zeros((3, HALO, cols), f32)

        def zero(i, carry):
            for c in range(STEPS):
                for f in range(4):
                    xh[c, 0, f, i] = jnp.zeros((8, width), f32)
            return carry

        lax.fori_loop(0, depth, zero, 0)

    @pl.when(jnp.logical_not(not_final))
    def _():
        hrecv[:, 0] = jnp.zeros_like(hrecv[:, 0])
        lr[:, rows : rows + HALO, :cols] = jnp.zeros((3, HALO, cols), f32)

        def zero(i, carry):
            for c in range(STEPS):
                for f in range(4):
                    xh[c, 1, f, i] = jnp.zeros((8, width), f32)
            return carry

        lax.fori_loop(0, depth, zero, 0)

    @pl.when(jnp.logical_not(band_low))
    def _():
        for c in range(STEPS):
            air[c, :, 0] = jnp.zeros((4, 8, width), f32)
        side[1] = jnp.zeros((3, full, 128), f32)

    @pl.when(jnp.logical_not(band_high))
    def _():
        for c in range(STEPS):
            air[c, :, depth + 1] = jnp.zeros((4, 8, width), f32)
        side[0] = jnp.zeros((3, full, 128), f32)

    @pl.when(jnp.logical_not(both(both(not_first, not_final), both(band_low, band_high))))
    def _():
        @pl.when(jnp.logical_not(not_first))
        def _():
            side[:, :, rows + HALO :] = jnp.zeros((2, 3, HALO, 128), f32)

        @pl.when(jnp.logical_not(not_final))
        def _():
            side[:, :, rows : rows + HALO] = jnp.zeros((2, 3, HALO, 128), f32)

    barrier = pltpu.get_barrier_semaphore()
    for tile_step, condition in ((0, None), (-1, not_first), (1, not_final)):
        for j in range(bands):
            ok = (band != j) if condition is None else condition

            @pl.when(ok)
            def _(tile_step=tile_step, j=j):
                pl.semaphore_signal(
                    barrier, inc=1, device_id=device(tile_step, j), device_id_type=MESH
                )

    row8 = lax.broadcasted_iota(jnp.int32, (8, width), 0)
    total_col = sum(math.exp(-k / LEVELS) for k in range(LEVELS))
    total_prof = sum(math.exp(-2.0 * k / LEVELS) for k in range(LEVELS))
    col_base = f32(0.0)
    prof_base = f32(0.0)
    for j in range(bands):
        here = band == j
        col_base = jnp.where(here, f32(math.exp(-j * depth / LEVELS) / total_col), col_base)
        prof_base = jnp.where(
            here, f32(LEVELS * math.exp(-2.0 * j * depth / LEVELS) / total_prof), prof_base
        )
    col_ratio = math.exp(-1.0 / LEVELS)
    prof_ratio = math.exp(-2.0 / LEVELS)

    def first_air(i, carry):
        weight, total_u, total_v = carry
        for f in range(4):
            air[0, f, i + 1] = air_in[f, i]
        total_u = total_u + weight * air_in[2, i]
        total_v = total_v + weight * air_in[3, i]
        return weight * f32(col_ratio), total_u, total_v

    nothing = jnp.zeros((8, width), f32)
    _, total_u, total_v = lax.fori_loop(0, depth, first_air, (col_base, nothing, nothing))

    def lookup(i, carry):
        at = pl.ds(pl.multiple_of(i * 8, 8), 8)
        kind = class_in[at, :]
        zero = jnp.zeros((8, cols), f32)
        rate, burn, hot, wet = zero, zero, zero, zero
        for k in range(NFUEL):
            same = kind == k
            rate = jnp.where(same, t_rate[k], rate)
            burn = jnp.where(same, t_burn[k], burn)
            hot = jnp.where(same, t_heat[k], hot)
            wet = jnp.where(same, t_moist[k], wet)
        lr[0, at, :cols] = level_in[at, :]
        lr[1, at, :cols] = rate
        lr[2, at, :cols] = ign_in[at, :].astype(f32)
        binv[at, :] = 1.0 / burn
        heat[at, :] = hot
        moist[at, :] = wet
        fuel_out[at, :] = fuel_in[at, :]
        return carry

    lax.fori_loop(0, chunks, lookup, 0)

    expected = (
        bands - 1 + bands * (not_first.astype(jnp.int32) + not_final.astype(jnp.int32))
    )
    pl.semaphore_wait(barrier, expected)

    def send_wind(c, total_u, total_v):
        stacked = jnp.concatenate([total_u, total_v], axis=0)
        row = lax.broadcasted_iota(jnp.int32, (8, 128), 0)
        for j in range(bands):
            shift = (128 // 4 - coarse * j) % width
            window = (pltpu.roll(stacked, shift, 1) if shift else stacked)[:, :128]
            wsend[c, j] = window
            turned = pltpu.roll(window[8:], 4, 0)
            hsend[c, 0, j] = jnp.where(row < 4, window[:8], turned)
            hsend[c, 1, j] = jnp.where(row >= 4, window[:8], turned)

            @pl.when(band == j)
            def _(window=window, j=j):
                wrecv[c, j] = window

        for j in range(bands):
            send(
                band != j,
                wsend.at[c, j],
                wrecv.at[c, band],
                wind_s.at[c, 2, j],
                wind_r.at[c, 2, band],
                device(0, j),
            )
        for way, tile_step, ok in ((0, -1, not_first), (1, 1, not_final)):
            for j in range(bands):
                send(
                    ok,
                    hsend.at[c, way, j],
                    hrecv.at[c, way, band],
                    wind_s.at[c, way, j],
                    wind_r.at[c, way, band],
                    device(tile_step, j),
                )

    def wait_wind(c):
        for j in range(bands):
            receive(band != j, wrecv.at[c, j], wind_r.at[c, 2, j], wind_s.at[c, 2, j], device(0, j))
        for way, tile_step, ok in ((0, 1, not_final), (1, -1, not_first)):
            for j in range(bands):
                receive(
                    ok,
                    hrecv.at[c, way, j],
                    wind_r.at[c, way, j],
                    wind_s.at[c, way, j],
                    device(tile_step, j),
                )

    def send_air(c):
        send(
            not_final,
            air.at[c, :, pl.ds(1, depth), pl.ds(7, 1), :],
            xh.at[c, 0, :, :, pl.ds(7, 1), :],
            halo_s.at[c, 0],
            halo_r.at[c, 0],
            device(1, band),
        )
        send(
            not_first,
            air.at[c, :, pl.ds(1, depth), pl.ds(0, 1), :],
            xh.at[c, 1, :, :, pl.ds(0, 1), :],
            halo_s.at[c, 1],
            halo_r.at[c, 1],
            device(-1, band),
        )
        send(
            band_high,
            air.at[c, :, depth],
            air.at[c, :, 0],
            halo_s.at[c, 2],
            halo_r.at[c, 2],
            device(0, band + 1),
        )
        send(
            band_low,
            air.at[c, :, 1],
            air.at[c, :, depth + 1],
            halo_s.at[c, 3],
            halo_r.at[c, 3],
            device(0, band - 1),
        )

    def wait_air(c):
        receive(
            not_first,
            xh.at[c, 0, :, :, pl.ds(7, 1), :],
            halo_r.at[c, 0],
            halo_s.at[c, 0],
            device(-1, band),
        )
        receive(
            not_final,
            xh.at[c, 1, :, :, pl.ds(0, 1), :],
            halo_r.at[c, 1],
            halo_s.at[c, 1],
            device(1, band),
        )
        receive(band_low, air.at[c, :, 0], halo_r.at[c, 2], halo_s.at[c, 2], device(0, band - 1))
        receive(
            band_high,
            air.at[c, :, depth + 1],
            halo_r.at[c, 3],
            halo_s.at[c, 3],
            device(0, band + 1),
        )

    send_wind(0, total_u, total_v)
    low_rows, high_rows = pl.ds(0, HALO), pl.ds(rows - HALO, HALO)
    own_rows = pl.ds(0, rows)
    from_next, from_last = pl.ds(rows, HALO), pl.ds(rows + HALO, HALO)
    low_cols, high_cols, own_cols = pl.ds(0, 128), pl.ds(cols - 128, 128), pl.ds(0, cols)
    index = 0
    waits = []
    for tile_step in (-1, 0, 1):
        for band_step in (-1, 0, 1):
            if tile_step == 0 and band_step == 0:
                continue
            src_rows = {-1: low_rows, 0: own_rows, 1: high_rows}[tile_step]
            dst_rows = {-1: from_next, 0: own_rows, 1: from_last}[tile_step]
            src_cols = {-1: low_cols, 0: own_cols, 1: high_cols}[band_step]
            if band_step == 0:
                dst = lr.at[:, dst_rows, own_cols]
            else:
                dst = side.at[0 if band_step < 0 else 1, :, dst_rows, :]
            tile_to = {-1: not_first, 0: None, 1: not_final}
            band_to = {-1: band_low, 0: None, 1: band_high}

            def joined(a, b):
                return b if a is None else (a if b is None else both(a, b))

            send(
                joined(tile_to[tile_step], band_to[band_step]),
                lr.at[:, src_rows, src_cols],
                dst,
                fire_s.at[index],
                fire_r.at[index],
                device(tile_step, band + band_step),
            )
            waits.append(
                (
                    joined(tile_to[-tile_step], band_to[-band_step]),
                    dst,
                    fire_r.at[index],
                    fire_s.at[index],
                    device(-tile_step, band - band_step),
                )
            )
            index += 1
    send_air(0)

    def iota(shape, dim):
        return lax.broadcasted_iota(jnp.int32, shape, dim)

    shape = (2 * full, 32)
    line, source = iota(shape, 0), iota(shape, 1)
    field = (line >= full).astype(jnp.int32)
    line = line - full * field
    own = both(
        line < rows,
        both(
            REFINE * (source - 8 * field) <= line,
            line < REFINE * (source - 8 * field) + REFINE,
        ),
    )
    after = both(
        both(line >= rows, line < rows + HALO),
        source == 16 + 4 * field + (line >= rows + REFINE).astype(jnp.int32),
    )
    before = both(
        line >= rows + HALO,
        source == 30 - 4 * field + (line >= rows + 2 * HALO - REFINE).astype(jnp.int32),
    )
    rx[...] = repeated(own | after | before, 1, 3)
    shape = (128, lanes)
    place, line = iota(shape, 0) - 32, iota(shape, 1)
    line = jnp.where(line < cols + 64, line, line - lanes)
    ry[...] = repeated(both(REFINE * place <= line, line < REFINE * place + REFINE), 0, 2)
    shape = (16, 2 * rows)
    place, line = iota(shape, 0), iota(shape, 1)
    sx[...] = repeated(both(REFINE * place <= line, line < REFINE * place + REFINE), 1, 3)
    shape = (cols, 128)
    line, place = iota(shape, 0), iota(shape, 1) - coarse * (band % 2)
    sy[...] = repeated(both(REFINE * place <= line, line < REFINE * place + REFINE), 0, 2)

    for wait in waits:
        receive(*wait)
    lane = iota((full, 128), 1)
    for k in range(3):
        lr[k, :, cols:] = jnp.where(lane < 64, side[0, k], side[1, k])
    lv[0] = lr[0]
    lv[1] = lr[0]

    row_f = iota((8, lanes), 0)
    lane_f = iota((8, lanes), 1)
    low_lane = jnp.where(band_low, -1, 0)
    high_lane = jnp.where(band_high, -1, cols - 1)

    def advance(src, i, fire_step, burn):
        at = pl.ds(pl.multiple_of(i * 8, 8), 8)
        last = pl.ds(pl.multiple_of(((i + all_chunks - 1) % all_chunks) * 8, 8), 8)
        following = pl.ds(pl.multiple_of(((i + 1) % all_chunks) * 8, 8), 8)
        here = lv[src, at, :]
        west = pltpu.roll(jnp.where(row_f == 7, lv[src, last, :], here), 1, 0)
        east = pltpu.roll(jnp.where(row_f == 0, lv[src, following, :], here), 7, 0)
        south = pltpu.roll(here, 1, 1)
        north = pltpu.roll(here, lanes - 1, 1)
        dw, de, ds, dn = here - west, east - here, here - south, north - here
        if burn:
            low_row = jnp.where(both(i == 0, jnp.logical_not(not_first)), 0, -1)
            high_row = jnp.where(both(i == chunks - 1, jnp.logical_not(not_final)), 7, -1)
            dw = jnp.where(row_f == low_row, 0.0, dw)
            de = jnp.where(row_f == high_row, 0.0, de)
        ds = jnp.where(lane_f == low_lane, 0.0, ds)
        dn = jnp.where(lane_f == high_lane, 0.0, dn)
        up_w, up_e = jnp.maximum(dw, 0.0), jnp.minimum(de, 0.0)
        up_s, up_n = jnp.maximum(ds, 0.0), jnp.minimum(dn, 0.0)
        square = (up_w * up_w + up_e * up_e) + (up_s * up_s + up_n * up_n)
        steep = square * lax.rsqrt(jnp.maximum(square, TINY))
        gx, gy = dw + de, ds + dn
        at_v = pl.ds(pl.multiple_of(full + i * 8, 8), 8)
        tail = (wind[at, :] * gx + wind[at_v, :] * gy) * lax.rsqrt(gx * gx + gy * gy + 4.0)
        speed = (fire_step * lr[1, at, :]) * (1.0 + 0.5 * jnp.maximum(tail, 0.0))
        new = here - speed * steep
        lv[1 - src, at, :] = new
        if burn:
            bsum[at, :] = bsum[at, :] + jnp.clip(0.5 - new[:, :cols], 0.0, 1.0)

    lane_a = lax.broadcasted_iota(jnp.int32, (8, width), 1)

    def write(c, f, i, value):
        if c == STEPS - 1:
            air_out[f, i] = value
        else:
            air[c + 1, f, i + 1] = value

    def move_air(c):
        wait_air(c)
        final = c == STEPS - 1

        def update(i, carry):
            weight, total_u, total_v = carry
            u, v = air[c, 2, i + 1], air[c, 3, i + 1]
            u_up, u_dn = jnp.maximum(u, 0.0), jnp.minimum(u, 0.0)
            v_up, v_dn = jnp.maximum(v, 0.0), jnp.minimum(v, 0.0)
            lift_x = lift_y = None
            for f in range(4):
                here = air[c, f, i + 1]
                west = pltpu.roll(jnp.where(row8 == 7, xh[c, 0, f, i], here), 1, 0)
                east = pltpu.roll(jnp.where(row8 == 0, xh[c, 1, f, i], here), 7, 0)
                south = jnp.where(lane_a == 0, 0.0, pltpu.roll(here, 1, 1))
                north = jnp.where(lane_a == width - 1, 0.0, pltpu.roll(here, width - 1, 1))
                dw, de, ds, dn = here - west, east - here, here - south, north - here
                advect = u_up * dw + u_dn * de + v_up * ds + v_dn * dn
                lap = (de - dw) + (dn - ds) + (
                    (air[c, f, i] + air[c, f, i + 2]) - 2.0 * here
                )
                new = here + 0.1 * (0.2 * lap - advect)
                if f == 0:
                    lift_x, lift_y = east - west, north - south
                elif f == 1:
                    lift_x = lift_x + 0.6 * (east - west)
                    lift_y = lift_y + 0.6 * (north - south)
                elif f == 2:
                    new = new + 0.015 * lift_x
                    total_u = total_u + weight * new
                else:
                    new = new + 0.015 * lift_y
                    total_v = total_v + weight * new
                write(c, f, i, new)
            return weight * f32(col_ratio), total_u, total_v

        _, total_u, total_v = lax.fori_loop(0, depth, update, (col_base, nothing, nothing), unroll=2)
        if not final:
            send_wind(c + 1, total_u, total_v)

    def finish_air(c):
        final = c == STEPS - 1
        for j in range(bands):
            receive(band != j, frecv.at[c, j], flux_r.at[c, j], flux_s.at[c, j], device(0, j))
        parts = [
            frecv[c, 2 * k] + frecv[c, 2 * k + 1] for k in range(width // 128)
        ]
        whole = jnp.concatenate(parts, axis=1)
        heat_in, moist_in = whole[:8], whole[8:]

        def force(i, weight):
            for f, flux in ((0, heat_in), (1, moist_in)):
                now = air_out[f, i] if final else air[c + 1, f, i + 1]
                write(c, f, i, now + weight * flux)
            return weight * f32(prof_ratio)

        lax.fori_loop(0, depth, force, prof_base * f32(2.0), unroll=2)

    for c in range(STEPS):
        fire_step = plan[c].astype(f32) * f32(0.15)

        def ignite(i, carry):
            at = pl.ds(pl.multiple_of(i * 8, 8), 8)
            now = lv[0, at, :]
            lv[0, at, :] = jnp.where(lr[2, at, :] <= float(c), jnp.minimum(now, -1.0), now)
            return carry

        lax.fori_loop(0, all_chunks, ignite, 0)
        bsum[...] = jnp.zeros_like(bsum)
        wait_wind(c)
        own = wrecv[c, 0]
        after = hrecv[c, 0, 0]
        before = hrecv[c, 1, 0]
        for j in range(1, bands):
            own = own + wrecv[c, j]
            after = after + hrecv[c, 0, j]
            before = before + hrecv[c, 1, j]
        together = jnp.concatenate([own, after, before], axis=0)
        wide = jnp.dot(split(together, 1, 2), ry[...], preferred_element_type=f32)
        wind[...] = jnp.dot(rx[...], split(wide, 0, 3), preferred_element_type=f32)

        near = (SUBSTEPS * (STEPS - c)) > 8

        def substep(src, fire_step=fire_step, near=near):
            def inner(i, carry):
                advance(src, i, fire_step, True)
                return carry

            lax.fori_loop(0, chunks, inner, 0, unroll=5)
            if near:

                def outer(i, carry):
                    advance(src, i, fire_step, False)
                    return carry

                lax.fori_loop(chunks, all_chunks, outer, 0, unroll=2)
            else:
                advance(src, chunks, fire_step, False)
                advance(src, all_chunks - 1, fire_step, False)

        substep(0)
        substep(1)
        if c % 2 == 0:
            move_air(c)
        else:
            finish_air(c - 1)
            send_air(c)
        substep(0)
        substep(1)

        def burn(i, carry):
            at = pl.ds(pl.multiple_of(i * 8, 8), 8)
            fuel = fuel_out[at, :]
            remain = fuel * jnp.exp(-fire_step * bsum[at, :] * binv[at, :])
            used = fuel - remain
            fuel_out[at, :] = remain
            ev[at, :] = used * heat[at, :]
            ev[pl.ds(pl.multiple_of(rows + i * 8, 8), 8), :] = used * moist[at, :]
            return carry

        lax.fori_loop(0, chunks, burn, 0)
        lines = jnp.dot(split(ev[...], 1, 2), sy[...], preferred_element_type=f32)
        flux = jnp.dot(sx[...], split(lines, 0, 3), preferred_element_type=f32)
        flux = flux * f32(1.0 / (REFINE * REFINE))
        fsend[c] = flux
        for j in range(bands):

            @pl.when(band == j)
            def _(j=j):
                frecv[c, j] = flux

            send(
                band != j,
                fsend.at[c],
                frecv.at[c, band],
                flux_s.at[c, j],
                flux_r.at[c, band],
                device(0, j),
            )
        if c % 2 == 1:
            move_air(c)
            finish_air(c)
            if c < STEPS - 1:
                send_air(c + 1)

    level_out[...] = lv[0, :rows, :cols]
    for condition, make in pending:

        @pl.when(condition)
        def _(make=make):
            make().wait_send()


def solution(mesh):
    tiles, sects, subs = (mesh.shape[name] for name in ("tile", "sect", "sub"))
    bands = sects * subs
    air_spec = P(None, ("sect", "sub"), ("group", "tile"), None)
    fire_spec = P(("group", "tile"), ("sect", "sub"))

    def local(air_state, fire_level, *rest):
        depth, width = air_state.shape[1], air_state.shape[3]
        rows, cols = fire_level.shape
        full, lanes = rows + 2 * HALO, cols + 128
        assert air_state.shape[2] == 8 and cols == 64 * REFINE and rows == 8 * REFINE
        vmem = pl.BlockSpec(memory_space=pltpu.VMEM)
        smem = pl.BlockSpec(memory_space=pltpu.SMEM)
        dma = pltpu.SemaphoreType.DMA
        return pl.pallas_call(
            functools.partial(kernel, tiles, sects, subs),
            out_shape=(
                jax.ShapeDtypeStruct(air_state.shape, f32),
                jax.ShapeDtypeStruct(fire_level.shape, f32),
                jax.ShapeDtypeStruct(fire_level.shape, f32),
            ),
            in_specs=[vmem] * 5 + [smem] * 5,
            out_specs=(vmem, vmem, vmem),
            scratch_shapes=[
                pltpu.VMEM((STEPS, 4, depth + 2, 8, width), f32),
                pltpu.VMEM((STEPS, 2, 4, depth, 8, width), f32),
                pltpu.VMEM((3, full, lanes), f32),
                pltpu.VMEM((2, 3, full, 128), f32),
                pltpu.VMEM((2, full, lanes), f32),
                pltpu.VMEM((rows, cols), f32),
                pltpu.VMEM((rows, cols), f32),
                pltpu.VMEM((rows, cols), f32),
                pltpu.VMEM((rows, cols), f32),
                pltpu.VMEM((2 * rows, cols), f32),
                pltpu.VMEM((2 * full, lanes), f32),
                pltpu.VMEM((2 * full, 96), bf16),
                pltpu.VMEM((256, lanes), bf16),
                pltpu.VMEM((16, 6 * rows), bf16),
                pltpu.VMEM((2 * cols, 128), bf16),
                pltpu.VMEM((STEPS, bands, 16, 128), f32),
                pltpu.VMEM((STEPS, bands, 16, 128), f32),
                pltpu.VMEM((STEPS, 2, bands, 8, 128), f32),
                pltpu.VMEM((STEPS, 2, bands, 8, 128), f32),
                pltpu.VMEM((STEPS, 16, 128), f32),
                pltpu.VMEM((STEPS, bands, 16, 128), f32),
                dma((8,)),
                dma((8,)),
                dma((STEPS, 3, bands)),
                dma((STEPS, 3, bands)),
                dma((STEPS, bands)),
                dma((STEPS, bands)),
                dma((STEPS, 4)),
                dma((STEPS, 4)),
            ],
            compiler_params=pltpu.CompilerParams(
                collective_id=0, has_side_effects=True, vmem_limit_bytes=56 * 1024 * 1024
            ),
        )(air_state, fire_level, *rest)

    return jax.shard_map(
        local,
        mesh=mesh,
        in_specs=(air_spec, fire_spec, fire_spec, fire_spec, fire_spec) + (P(),) * 5,
        out_specs=(air_spec, fire_spec, fire_spec),
        check_vma=False,
    )
```

```python
import functools
import math

import jax
import jax.numpy as jnp
from jax import lax
from jax.experimental import pallas as pl
from jax.experimental.pallas import tpu as pltpu
from jax.sharding import PartitionSpec as P

LEVELS = 80
REFINE = 10
NFUEL = 13
STEPS = 4
SUBSTEPS = 4
HALO = STEPS * SUBSTEPS
MESH = pl.DeviceIdType.MESH
TINY = 1.1754944e-38
f32 = jnp.float32
bf16 = jnp.bfloat16


def split(value, axis, pieces):
    parts = []
    for _ in range(pieces):
        parts.append(value.astype(bf16))
        value = value - parts[-1].astype(f32)
    return jnp.concatenate(parts, axis=axis)


def repeated(mask, axis, pieces):
    return jnp.concatenate([jnp.where(mask, 1.0, 0.0).astype(bf16)] * pieces, axis=axis)


def kernel(
    tiles,
    sects,
    subs,
    air_in,
    level_in,
    fuel_in,
    class_in,
    ign_in,
    plan,
    t_rate,
    t_burn,
    t_heat,
    t_moist,
    air_out,
    level_out,
    fuel_out,
    air,
    xh,
    lr,
    side,
    lv,
    bsum,
    binv,
    heat,
    moist,
    ev,
    wind,
    rx,
    ry,
    sx,
    sy,
    wsend,
    wrecv,
    hsend,
    hrecv,
    fsend,
    frecv,
    fire_s,
    fire_r,
    wind_s,
    wind_r,
    flux_s,
    flux_r,
    halo_s,
    halo_r,
):
    bands = sects * subs
    depth = air_in.shape[1]
    width = air_in.shape[3]
    rows, cols = level_in.shape
    full = rows + 2 * HALO
    lanes = cols + 128
    chunks = rows // 8
    all_chunks = full // 8
    coarse = cols // REFINE
    tile_at = lax.axis_index("tile")
    sect_at = lax.axis_index("sect")
    sub_at = lax.axis_index("sub")
    band = sect_at * subs + sub_at
    not_first = tile_at > 0
    not_final = tile_at < tiles - 1
    band_low = band > 0
    band_high = band < bands - 1

    def device(tile_step, at_band):
        return {
            "tile": tile_at + tile_step,
            "sect": at_band // subs,
            "sub": at_band % subs,
        }

    def both(a, b):
        return jnp.logical_and(a, b)

    pending = []

    def send(condition, src, dst, send_sem, recv_sem, where):
        def make():
            return pltpu.make_async_remote_copy(
                src_ref=src,
                dst_ref=dst,
                send_sem=send_sem,
                recv_sem=recv_sem,
                device_id=where,
                device_id_type=MESH,
            )

        @pl.when(condition)
        def _():
            make().start()

        pending.append((condition, make))

    def receive(condition, dst, recv_sem, send_sem, where):
        @pl.when(condition)
        def _():
            pltpu.make_async_remote_copy(
                src_ref=dst,
                dst_ref=dst,
                send_sem=send_sem,
                recv_sem=recv_sem,
                device_id=where,
                device_id_type=MESH,
            ).wait_recv()

    @pl.when(jnp.logical_not(not_first))
    def _():
        hrecv[:, 1] = jnp.zeros_like(hrecv[:, 1])
        lr[:, rows + HALO :, :cols] = jnp.zeros((3, HALO, cols), f32)

        def zero(i, carry):
            for c in range(STEPS):
                for f in range(4):
                    xh[c, 0, f, i] = jnp.zeros((8, width), f32)
            return carry

        lax.fori_loop(0, depth, zero, 0)

    @pl.when(jnp.logical_not(not_final))
    def _():
        hrecv[:, 0] = jnp.zeros_like(hrecv[:, 0])
        lr[:, rows : rows + HALO, :cols] = jnp.zeros((3, HALO, cols), f32)

        def zero(i, carry):
            for c in range(STEPS):
                for f in range(4):
                    xh[c, 1, f, i] = jnp.zeros((8, width), f32)
            return carry

        lax.fori_loop(0, depth, zero, 0)

    @pl.when(jnp.logical_not(band_low))
    def _():
        for c in range(STEPS):
            air[c, :, 0] = jnp.zeros((4, 8, width), f32)
        side[1] = jnp.zeros((3, full, 128), f32)

    @pl.when(jnp.logical_not(band_high))
    def _():
        for c in range(STEPS):
            air[c, :, depth + 1] = jnp.zeros((4, 8, width), f32)
        side[0] = jnp.zeros((3, full, 128), f32)

    @pl.when(jnp.logical_not(both(both(not_first, not_final), both(band_low, band_high))))
    def _():
        @pl.when(jnp.logical_not(not_first))
        def _():
            side[:, :, rows + HALO :] = jnp.zeros((2, 3, HALO, 128), f32)

        @pl.when(jnp.logical_not(not_final))
        def _():
            side[:, :, rows : rows + HALO] = jnp.zeros((2, 3, HALO, 128), f32)

    barrier = pltpu.get_barrier_semaphore()
    for tile_step, condition in ((0, None), (-1, not_first), (1, not_final)):
        for j in range(bands):
            ok = (band != j) if condition is None else condition

            @pl.when(ok)
            def _(tile_step=tile_step, j=j):
                pl.semaphore_signal(
                    barrier, inc=1, device_id=device(tile_step, j), device_id_type=MESH
                )

    row8 = lax.broadcasted_iota(jnp.int32, (8, width), 0)
    total_col = sum(math.exp(-k / LEVELS) for k in range(LEVELS))
    total_prof = sum(math.exp(-2.0 * k / LEVELS) for k in range(LEVELS))
    col_base = f32(0.0)
    prof_base = f32(0.0)
    for j in range(bands):
        here = band == j
        col_base = jnp.where(here, f32(math.exp(-j * depth / LEVELS) / total_col), col_base)
        prof_base = jnp.where(
            here, f32(LEVELS * math.exp(-2.0 * j * depth / LEVELS) / total_prof), prof_base
        )
    col_ratio = math.exp(-1.0 / LEVELS)
    prof_ratio = math.exp(-2.0 / LEVELS)

    def first_air(i, carry):
        weight, total_u, total_v = carry
        for f in range(4):
            air[0, f, i + 1] = air_in[f, i]
        total_u = total_u + weight * air_in[2, i]
        total_v = total_v + weight * air_in[3, i]
        return weight * f32(col_ratio), total_u, total_v

    nothing = jnp.zeros((8, width), f32)
    _, total_u, total_v = lax.fori_loop(0, depth, first_air, (col_base, nothing, nothing))

    def lookup(i, carry):
        at = pl.ds(pl.multiple_of(i * 8, 8), 8)
        kind = class_in[at, :]
        zero = jnp.zeros((8, cols), f32)
        rate, burn, hot, wet = zero, zero, zero, zero
        for k in range(NFUEL):
            same = kind == k
            rate = jnp.where(same, t_rate[k], rate)
            burn = jnp.where(same, t_burn[k], burn)
            hot = jnp.where(same, t_heat[k], hot)
            wet = jnp.where(same, t_moist[k], wet)
        lr[0, at, :cols] = level_in[at, :]
        lr[1, at, :cols] = rate
        lr[2, at, :cols] = ign_in[at, :].astype(f32)
        binv[at, :] = 1.0 / burn
        heat[at, :] = hot
        moist[at, :] = wet
        fuel_out[at, :] = fuel_in[at, :]
        return carry

    lax.fori_loop(0, chunks, lookup, 0)

    expected = (
        bands - 1 + bands * (not_first.astype(jnp.int32) + not_final.astype(jnp.int32))
    )
    pl.semaphore_wait(barrier, expected)

    def send_wind(c, total_u, total_v):
        stacked = jnp.concatenate([total_u, total_v], axis=0)
        row = lax.broadcasted_iota(jnp.int32, (8, 128), 0)
        for j in range(bands):
            shift = (128 // 4 - coarse * j) % width
            window = (pltpu.roll(stacked, shift, 1) if shift else stacked)[:, :128]
            wsend[c, j] = window
            turned = pltpu.roll(window[8:], 4, 0)
            hsend[c, 0, j] = jnp.where(row < 4, window[:8], turned)
            hsend[c, 1, j] = jnp.where(row >= 4, window[:8], turned)

            @pl.when(band == j)
            def _(window=window, j=j):
                wrecv[c, j] = window

        for j in range(bands):
            send(
                band != j,
                wsend.at[c, j],
                wrecv.at[c, band],
                wind_s.at[c, 2, j],
                wind_r.at[c, 2, band],
                device(0, j),
            )
        for way, tile_step, ok in ((0, -1, not_first), (1, 1, not_final)):
            for j in range(bands):
                send(
                    ok,
                    hsend.at[c, way, j],
                    hrecv.at[c, way, band],
                    wind_s.at[c, way, j],
                    wind_r.at[c, way, band],
                    device(tile_step, j),
                )

    def wait_wind(c):
        for j in range(bands):
            receive(band != j, wrecv.at[c, j], wind_r.at[c, 2, j], wind_s.at[c, 2, j], device(0, j))
        for way, tile_step, ok in ((0, 1, not_final), (1, -1, not_first)):
            for j in range(bands):
                receive(
                    ok,
                    hrecv.at[c, way, j],
                    wind_r.at[c, way, j],
                    wind_s.at[c, way, j],
                    device(tile_step, j),
                )

    def send_air(c):
        send(
            not_final,
            air.at[c, :, pl.ds(1, depth), pl.ds(7, 1), :],
            xh.at[c, 0, :, :, pl.ds(7, 1), :],
            halo_s.at[c, 0],
            halo_r.at[c, 0],
            device(1, band),
        )
        send(
            not_first,
            air.at[c, :, pl.ds(1, depth), pl.ds(0, 1), :],
            xh.at[c, 1, :, :, pl.ds(0, 1), :],
            halo_s.at[c, 1],
            halo_r.at[c, 1],
            device(-1, band),
        )
        send(
            band_high,
            air.at[c, :, depth],
            air.at[c, :, 0],
            halo_s.at[c, 2],
            halo_r.at[c, 2],
            device(0, band + 1),
        )
        send(
            band_low,
            air.at[c, :, 1],
            air.at[c, :, depth + 1],
            halo_s.at[c, 3],
            halo_r.at[c, 3],
            device(0, band - 1),
        )

    def wait_air(c):
        receive(
            not_first,
            xh.at[c, 0, :, :, pl.ds(7, 1), :],
            halo_r.at[c, 0],
            halo_s.at[c, 0],
            device(-1, band),
        )
        receive(
            not_final,
            xh.at[c, 1, :, :, pl.ds(0, 1), :],
            halo_r.at[c, 1],
            halo_s.at[c, 1],
            device(1, band),
        )
        receive(band_low, air.at[c, :, 0], halo_r.at[c, 2], halo_s.at[c, 2], device(0, band - 1))
        receive(
            band_high,
            air.at[c, :, depth + 1],
            halo_r.at[c, 3],
            halo_s.at[c, 3],
            device(0, band + 1),
        )

    send_wind(0, total_u, total_v)
    send_air(0)
    low_rows, high_rows = pl.ds(0, HALO), pl.ds(rows - HALO, HALO)
    own_rows = pl.ds(0, rows)
    from_next, from_last = pl.ds(rows, HALO), pl.ds(rows + HALO, HALO)
    low_cols, high_cols, own_cols = pl.ds(0, 128), pl.ds(cols - 128, 128), pl.ds(0, cols)
    index = 0
    waits = []
    for tile_step in (-1, 0, 1):
        for band_step in (-1, 0, 1):
            if tile_step == 0 and band_step == 0:
                continue
            src_rows = {-1: low_rows, 0: own_rows, 1: high_rows}[tile_step]
            dst_rows = {-1: from_next, 0: own_rows, 1: from_last}[tile_step]
            src_cols = {-1: low_cols, 0: own_cols, 1: high_cols}[band_step]
            if band_step == 0:
                dst = lr.at[:, dst_rows, own_cols]
            else:
                dst = side.at[0 if band_step < 0 else 1, :, dst_rows, :]
            tile_to = {-1: not_first, 0: None, 1: not_final}
            band_to = {-1: band_low, 0: None, 1: band_high}

            def joined(a, b):
                return b if a is None else (a if b is None else both(a, b))

            send(
                joined(tile_to[tile_step], band_to[band_step]),
                lr.at[:, src_rows, src_cols],
                dst,
                fire_s.at[index],
                fire_r.at[index],
                device(tile_step, band + band_step),
            )
            waits.append(
                (
                    joined(tile_to[-tile_step], band_to[-band_step]),
                    dst,
                    fire_r.at[index],
                    fire_s.at[index],
                    device(-tile_step, band - band_step),
                )
            )
            index += 1

    def iota(shape, dim):
        return lax.broadcasted_iota(jnp.int32, shape, dim)

    shape = (2 * full, 32)
    line, source = iota(shape, 0), iota(shape, 1)
    field = (line >= full).astype(jnp.int32)
    line = line - full * field
    own = both(
        line < rows,
        both(
            REFINE * (source - 8 * field) <= line,
            line < REFINE * (source - 8 * field) + REFINE,
        ),
    )
    after = both(
        both(line >= rows, line < rows + HALO),
        source == 16 + 4 * field + (line >= rows + REFINE).astype(jnp.int32),
    )
    before = both(
        line >= rows + HALO,
        source == 30 - 4 * field + (line >= rows + 2 * HALO - REFINE).astype(jnp.int32),
    )
    rx[...] = repeated(own | after | before, 1, 3)
    shape = (128, lanes)
    place, line = iota(shape, 0) - 32, iota(shape, 1)
    line = jnp.where(line < cols + 64, line, line - lanes)
    ry[...] = repeated(both(REFINE * place <= line, line < REFINE * place + REFINE), 0, 2)
    shape = (16, 2 * rows)
    place, line = iota(shape, 0), iota(shape, 1)
    sx[...] = repeated(both(REFINE * place <= line, line < REFINE * place + REFINE), 1, 3)
    shape = (cols, 128)
    line, place = iota(shape, 0), iota(shape, 1) - coarse * (band % 2)
    sy[...] = repeated(both(REFINE * place <= line, line < REFINE * place + REFINE), 0, 2)

    row_f = iota((8, lanes), 0)
    lane_f = iota((8, lanes), 1)
    low_lane = jnp.where(band_low, -1, 0)
    high_lane = jnp.where(band_high, -1, cols - 1)

    def advance(src, i, fire_step, burn):
        at = pl.ds(pl.multiple_of(i * 8, 8), 8)
        last = pl.ds(pl.multiple_of(((i + all_chunks - 1) % all_chunks) * 8, 8), 8)
        following = pl.ds(pl.multiple_of(((i + 1) % all_chunks) * 8, 8), 8)
        here = lv[src, at, :]
        west = pltpu.roll(jnp.where(row_f == 7, lv[src, last, :], here), 1, 0)
        east = pltpu.roll(jnp.where(row_f == 0, lv[src, following, :], here), 7, 0)
        south = pltpu.roll(here, 1, 1)
        north = pltpu.roll(here, lanes - 1, 1)
        dw, de, ds, dn = here - west, east - here, here - south, north - here
        if burn:
            low_row = jnp.where(both(i == 0, jnp.logical_not(not_first)), 0, -1)
            high_row = jnp.where(both(i == chunks - 1, jnp.logical_not(not_final)), 7, -1)
            dw = jnp.where(row_f == low_row, 0.0, dw)
            de = jnp.where(row_f == high_row, 0.0, de)
        ds = jnp.where(lane_f == low_lane, 0.0, ds)
        dn = jnp.where(lane_f == high_lane, 0.0, dn)
        up_w, up_e = jnp.maximum(dw, 0.0), jnp.minimum(de, 0.0)
        up_s, up_n = jnp.maximum(ds, 0.0), jnp.minimum(dn, 0.0)
        square = (up_w * up_w + up_e * up_e) + (up_s * up_s + up_n * up_n)
        steep = square * lax.rsqrt(jnp.maximum(square, TINY))
        gx, gy = dw + de, ds + dn
        at_v = pl.ds(pl.multiple_of(full + i * 8, 8), 8)
        tail = (wind[at, :] * gx + wind[at_v, :] * gy) * lax.rsqrt(gx * gx + gy * gy + 4.0)
        speed = (fire_step * lr[1, at, :]) * (1.0 + 0.5 * jnp.maximum(tail, 0.0))
        new = here - speed * steep
        lv[1 - src, at, :] = new
        if burn:
            bsum[at, :] = bsum[at, :] + jnp.clip(0.5 - new[:, :cols], 0.0, 1.0)

    lane_a = lax.broadcasted_iota(jnp.int32, (8, width), 1)

    def write(c, f, i, value):
        if c == STEPS - 1:
            air_out[f, i] = value
        else:
            air[c + 1, f, i + 1] = value

    def move_air(c):
        wait_air(c)
        final = c == STEPS - 1

        def update(i, carry):
            weight, total_u, total_v = carry
            u, v = air[c, 2, i + 1], air[c, 3, i + 1]
            u_up, u_dn = jnp.maximum(u, 0.0), jnp.minimum(u, 0.0)
            v_up, v_dn = jnp.maximum(v, 0.0), jnp.minimum(v, 0.0)
            lift_x = lift_y = None
            for f in range(4):
                here = air[c, f, i + 1]
                west = pltpu.roll(jnp.where(row8 == 7, xh[c, 0, f, i], here), 1, 0)
                east = pltpu.roll(jnp.where(row8 == 0, xh[c, 1, f, i], here), 7, 0)
                south = jnp.where(lane_a == 0, 0.0, pltpu.roll(here, 1, 1))
                north = jnp.where(lane_a == width - 1, 0.0, pltpu.roll(here, width - 1, 1))
                dw, de, ds, dn = here - west, east - here, here - south, north - here
                advect = u_up * dw + u_dn * de + v_up * ds + v_dn * dn
                lap = (de - dw) + (dn - ds) + (
                    (air[c, f, i] + air[c, f, i + 2]) - 2.0 * here
                )
                new = here + 0.1 * (0.2 * lap - advect)
                if f == 0:
                    lift_x, lift_y = east - west, north - south
                elif f == 1:
                    lift_x = lift_x + 0.6 * (east - west)
                    lift_y = lift_y + 0.6 * (north - south)
                elif f == 2:
                    new = new + 0.015 * lift_x
                    total_u = total_u + weight * new
                else:
                    new = new + 0.015 * lift_y
                    total_v = total_v + weight * new
                write(c, f, i, new)
            return weight * f32(col_ratio), total_u, total_v

        _, total_u, total_v = lax.fori_loop(0, depth, update, (col_base, nothing, nothing), unroll=2)
        if not final:
            send_wind(c + 1, total_u, total_v)

    def finish_air(c):
        final = c == STEPS - 1
        for j in range(bands):
            receive(band != j, frecv.at[c, j], flux_r.at[c, j], flux_s.at[c, j], device(0, j))
        parts = [
            frecv[c, 2 * k] + frecv[c, 2 * k + 1] for k in range(width // 128)
        ]
        whole = jnp.concatenate(parts, axis=1)
        heat_in, moist_in = whole[:8], whole[8:]

        def force(i, weight):
            for f, flux in ((0, heat_in), (1, moist_in)):
                now = air_out[f, i] if final else air[c + 1, f, i + 1]
                write(c, f, i, now + weight * flux)
            return weight * f32(prof_ratio)

        lax.fori_loop(0, depth, force, prof_base * f32(2.0), unroll=2)

    move_air(0)
    for wait in waits:
        receive(*wait)
    lane = iota((full, 128), 1)
    for k in range(3):
        lr[k, :, cols:] = jnp.where(lane < 64, side[0, k], side[1, k])
    lv[0] = lr[0]
    lv[1] = lr[0]

    for c in range(STEPS):
        fire_step = plan[c].astype(f32) * f32(0.15)

        def ignite(i, carry):
            at = pl.ds(pl.multiple_of(i * 8, 8), 8)
            now = lv[0, at, :]
            lv[0, at, :] = jnp.where(lr[2, at, :] <= float(c), jnp.minimum(now, -1.0), now)
            return carry

        lax.fori_loop(0, all_chunks, ignite, 0)
        bsum[...] = jnp.zeros_like(bsum)
        wait_wind(c)
        own = wrecv[c, 0]
        after = hrecv[c, 0, 0]
        before = hrecv[c, 1, 0]
        for j in range(1, bands):
            own = own + wrecv[c, j]
            after = after + hrecv[c, 0, j]
            before = before + hrecv[c, 1, j]
        together = jnp.concatenate([own, after, before], axis=0)
        wide = jnp.dot(split(together, 1, 2), ry[...], preferred_element_type=f32)
        wind[...] = jnp.dot(rx[...], split(wide, 0, 3), preferred_element_type=f32)

        near = (SUBSTEPS * (STEPS - c)) > 8

        def substep(src, fire_step=fire_step, near=near):
            def inner(i, carry):
                advance(src, i, fire_step, True)
                return carry

            lax.fori_loop(0, chunks, inner, 0, unroll=5)
            if near:

                def outer(i, carry):
                    advance(src, i, fire_step, False)
                    return carry

                lax.fori_loop(chunks, all_chunks, outer, 0, unroll=2)
            else:
                advance(src, chunks, fire_step, False)
                advance(src, all_chunks - 1, fire_step, False)

        substep(0)
        substep(1)
        if c % 2 == 0 and c > 0:
            move_air(c)
        elif c % 2 == 1:
            finish_air(c - 1)
            send_air(c)
        substep(0)
        substep(1)

        def burn(i, carry):
            at = pl.ds(pl.multiple_of(i * 8, 8), 8)
            fuel = fuel_out[at, :]
            remain = fuel * jnp.exp(-fire_step * bsum[at, :] * binv[at, :])
            used = fuel - remain
            fuel_out[at, :] = remain
            ev[at, :] = used * heat[at, :]
            ev[pl.ds(pl.multiple_of(rows + i * 8, 8), 8), :] = used * moist[at, :]
            return carry

        lax.fori_loop(0, chunks, burn, 0)
        lines = jnp.dot(split(ev[...], 1, 2), sy[...], preferred_element_type=f32)
        flux = jnp.dot(sx[...], split(lines, 0, 3), preferred_element_type=f32)
        flux = flux * f32(1.0 / (REFINE * REFINE))
        fsend[c] = flux
        for j in range(bands):

            @pl.when(band == j)
            def _(j=j):
                frecv[c, j] = flux

            send(
                band != j,
                fsend.at[c],
                frecv.at[c, band],
                flux_s.at[c, j],
                flux_r.at[c, band],
                device(0, j),
            )
        if c % 2 == 1:
            move_air(c)
            finish_air(c)
            if c < STEPS - 1:
                send_air(c + 1)

    level_out[...] = lv[0, :rows, :cols]
    for condition, make in pending:

        @pl.when(condition)
        def _(make=make):
            make().wait_send()


def solution(mesh):
    tiles, sects, subs = (mesh.shape[name] for name in ("tile", "sect", "sub"))
    bands = sects * subs
    air_spec = P(None, ("sect", "sub"), ("group", "tile"), None)
    fire_spec = P(("group", "tile"), ("sect", "sub"))

    def local(air_state, fire_level, *rest):
        depth, width = air_state.shape[1], air_state.shape[3]
        rows, cols = fire_level.shape
        full, lanes = rows + 2 * HALO, cols + 128
        assert air_state.shape[2] == 8 and cols == 64 * REFINE and rows == 8 * REFINE
        vmem = pl.BlockSpec(memory_space=pltpu.VMEM)
        smem = pl.BlockSpec(memory_space=pltpu.SMEM)
        dma = pltpu.SemaphoreType.DMA
        return pl.pallas_call(
            functools.partial(kernel, tiles, sects, subs),
            out_shape=(
                jax.ShapeDtypeStruct(air_state.shape, f32),
                jax.ShapeDtypeStruct(fire_level.shape, f32),
                jax.ShapeDtypeStruct(fire_level.shape, f32),
            ),
            in_specs=[vmem] * 5 + [smem] * 5,
            out_specs=(vmem, vmem, vmem),
            scratch_shapes=[
                pltpu.VMEM((STEPS, 4, depth + 2, 8, width), f32),
                pltpu.VMEM((STEPS, 2, 4, depth, 8, width), f32),
                pltpu.VMEM((3, full, lanes), f32),
                pltpu.VMEM((2, 3, full, 128), f32),
                pltpu.VMEM((2, full, lanes), f32),
                pltpu.VMEM((rows, cols), f32),
                pltpu.VMEM((rows, cols), f32),
                pltpu.VMEM((rows, cols), f32),
                pltpu.VMEM((rows, cols), f32),
                pltpu.VMEM((2 * rows, cols), f32),
                pltpu.VMEM((2 * full, lanes), f32),
                pltpu.VMEM((2 * full, 96), bf16),
                pltpu.VMEM((256, lanes), bf16),
                pltpu.VMEM((16, 6 * rows), bf16),
                pltpu.VMEM((2 * cols, 128), bf16),
                pltpu.VMEM((STEPS, bands, 16, 128), f32),
                pltpu.VMEM((STEPS, bands, 16, 128), f32),
                pltpu.VMEM((STEPS, 2, bands, 8, 128), f32),
                pltpu.VMEM((STEPS, 2, bands, 8, 128), f32),
                pltpu.VMEM((STEPS, 16, 128), f32),
                pltpu.VMEM((STEPS, bands, 16, 128), f32),
                dma((8,)),
                dma((8,)),
                dma((STEPS, 3, bands)),
                dma((STEPS, 3, bands)),
                dma((STEPS, bands)),
                dma((STEPS, bands)),
                dma((STEPS, 4)),
                dma((STEPS, 4)),
            ],
            compiler_params=pltpu.CompilerParams(
                collective_id=0, has_side_effects=True, vmem_limit_bytes=56 * 1024 * 1024
            ),
        )(air_state, fire_level, *rest)

    return jax.shard_map(
        local,
        mesh=mesh,
        in_specs=(air_spec, fire_spec, fire_spec, fire_spec, fire_spec) + (P(),) * 5,
        out_specs=(air_spec, fire_spec, fire_spec),
        check_vma=False,
    )
```
